256 devices in a mesh: tm: 32 (over y, z), space: 8 (over x, core).
Axes of the slice: x: 4, y: 4, z: 8, core: 2. Of those that a mesh axis runs over, the one named last changes fastest.
Arguments:
- start_states: float32 [32, 3, 16, 128, 256], P('tm', None, None, 'space'), may hold values from -6 to 6
- labels: int32 [16, 128, 256], P(None, 'space'), may hold values 0 or 1
Outputs:
- next_states: float32 [32, 3, 16, 128, 256], P('tm', None, None, 'space')
The draws below stay inside these ranges and needn't reach their ends.
All inputs are finite; a program needn't handle non-finite values. No bound on the sum of `labels` on one device may be relied on, other than what follows from the above.
Results may differ from the reference program's by a relative error of at most 0.0001.
Values sent between devices are 32-bit elements; how exact they have to be, the bound alone decides.
No kernel may reach another device: no remote copies, remote signals or barrier semaphores. Data moves between devices by JAX's collectives and lax.ppermute only.
A program may use at most 128 MiB of HBM per device.

```python
import math
import jax
import jax.numpy as jnp
from jax import lax

NZ = 16
NY = 256
VCYCLES = 2
COARSE_SWEEPS = 4
NX = 128
N_TM = 32


def draw_start_states(key, part):
    keys = jax.random.split(jax.random.fold_in(key, 11), 3)
    columns = jnp.arange(NX, dtype=jnp.float32).reshape(1, 1, 1, NX, 1)
    phase = jax.random.uniform(keys[0], (N_TM, 3, 1, 1, 1), jnp.float32, 0.0, 2.0 * math.pi)
    sign = jnp.where(jax.random.bernoulli(keys[2], 0.5, (N_TM, 3, 1, 1, 1)), 1.0, -1.0).astype(jnp.float32)
    level = 1.5
    amplitude = 3.0
    coarse_noise = 0.7 * jnp.clip(jax.random.normal(keys[1], (N_TM, 3, NZ // 2, NX // 2, NY // 2), jnp.float32), -2.0, 2.0)
    noise = jnp.repeat(jnp.repeat(jnp.repeat(coarse_noise, 2, axis=2), 2, axis=3), 2, axis=4)
    wave = amplitude * jnp.sin(2.0 * math.pi * columns / 32.0 + phase)
    smooth = sign * level + wave
    return (jnp.broadcast_to(smooth, (N_TM, 3, NZ, NX, NY)) + noise).astype(jnp.float32)


def touch_ends(array, stream_key, smallest, top_value):
    dims = array.shape
    index_at = [jax.random.randint(jax.random.fold_in(stream_key, axis), (), 0, dims[axis]) for axis in range(len(dims))]
    array = array.at[tuple(index_at)].set(smallest)
    longest = dims.index(max(dims))
    index_at[longest] = (index_at[longest] + 1) % dims[longest]
    return array.at[tuple(index_at)].set(top_value)


def setup_inputs(seed: int = 0) -> dict:
    key_list = jax.random.split(jax.random.key(seed), 3)
    return {
        "start_states": draw_start_states(jax.random.fold_in(key_list[2], 71), 0),
        "labels": touch_ends((jax.random.randint(key_list[1], (NZ, NX, NY), 0, 20) < 1).astype(jnp.int32), jax.random.fold_in(key_list[1], 1), 0, 1),
    }


viscosity = 0.1
buoyancy = 0.2
relaxation = 0.8
coarse_rate = 0.15


def neighbour(values, direction, offset):
    position = values.ndim + direction
    padding = [(0, 0)] * values.ndim
    padding[position] = (1, 1)
    padded = jnp.pad(values, padding)
    length = values.shape[position]
    return lax.slice_in_dim(padded, 1 + offset, 1 + offset + length, axis=position)


def restrict(values):
    leading = values.shape[:-3]
    depth_cells, across_cells, height_cells = values.shape[-3:]
    shaped = values.reshape(leading + (depth_cells // 2, 2, across_cells // 2, 2, height_cells // 2, 2))
    return jnp.mean(shaped, axis=(-5, -3, -1))


def prolong(values):
    return jnp.repeat(jnp.repeat(jnp.repeat(values, 2, axis=-3), 2, axis=-2), 2, axis=-1)


def laplace_with(values, upper_across, lower_across):
    summed = neighbour(values, -3, 1) + neighbour(values, -3, -1) + upper_across + lower_across
    summed = summed + neighbour(values, -1, 1) + neighbour(values, -1, -1)
    return summed - 6.0 * values


def laplace(values):
    return laplace_with(values, neighbour(values, -2, 1), neighbour(values, -2, -1))


def face_weights(mobility, upper_across, lower_across):
    return ((0.5 * (mobility + neighbour(mobility, -3, 1)), 0.5 * (mobility + neighbour(mobility, -3, -1))),
            (0.5 * (mobility + upper_across), 0.5 * (mobility + lower_across)),
            (0.5 * (mobility + neighbour(mobility, -1, 1)), 0.5 * (mobility + neighbour(mobility, -1, -1))))


def scaled_weights(weights):
    return tuple((0.25 * upper_face, 0.25 * lower_face) for upper_face, lower_face in weights)


def weight_sum(weights):
    summed = weights[0][0] + weights[0][1]
    for upper_face, lower_face in weights[1:]:
        summed = summed + upper_face + lower_face
    return summed


def apply_weights(values, upper_across, lower_across, weights):
    depth_pair, across_pair, height_pair = weights
    summed = depth_pair[0] * (values - neighbour(values, -3, 1)) + depth_pair[1] * (values - neighbour(values, -3, -1))
    summed = summed + across_pair[0] * (values - upper_across) + across_pair[1] * (values - lower_across)
    return summed + height_pair[0] * (values - neighbour(values, -1, 1)) + height_pair[1] * (values - neighbour(values, -1, -1))


def operate(values, weights):
    return apply_weights(values, neighbour(values, -2, 1), neighbour(values, -2, -1), weights)


def vcycle(pressure, target, weights, diagonal, coarse_weights, coarse_diagonal):
    pressure = pressure + relaxation * (target - operate(pressure, weights)) / diagonal
    leftover = restrict(target - operate(pressure, weights))
    correction = relaxation * leftover / coarse_diagonal
    for sweep_number in range(COARSE_SWEEPS - 1):
        correction = correction + relaxation * (leftover - operate(correction, coarse_weights)) / coarse_diagonal
    pressure = pressure + prolong(correction)
    return pressure + relaxation * (target - operate(pressure, weights)) / diagonal


def fine_step(initial, mobility, weights, diagonal, coarse_weights, coarse_diagonal):
    zeros_field = jnp.zeros_like(mobility)
    predicted = initial + viscosity * laplace(initial) + jnp.stack([buoyancy * (2.0 * mobility - 1.0), zeros_field, zeros_field])
    spread = (neighbour(predicted[0], -3, 1) - neighbour(predicted[0], -3, -1)) + (neighbour(predicted[1], -2, 1) - neighbour(predicted[1], -2, -1))
    spread = spread + (neighbour(predicted[2], -1, 1) - neighbour(predicted[2], -1, -1))
    target = -0.5 * spread
    pressure = jnp.zeros_like(mobility)
    for cycle_number in range(VCYCLES):
        pressure = vcycle(pressure, target, weights, diagonal, coarse_weights, coarse_diagonal)
    gradient = jnp.stack([0.5 * (neighbour(pressure, -3, 1) - neighbour(pressure, -3, -1)),
                          0.5 * (neighbour(pressure, -2, 1) - neighbour(pressure, -2, -1)),
                          0.5 * (neighbour(pressure, -1, 1) - neighbour(pressure, -1, -1))])
    return predicted - mobility * gradient


def coarse_step(values, mobility_coarse):
    for substep in range(2):
        values = values + coarse_rate * mobility_coarse * laplace(values)
    return values


def reference(start_states, labels):
    mobility = 1.0 / (1.0 + 3.0 * labels.astype(jnp.float32))
    weights = face_weights(mobility, neighbour(mobility, -2, 1), neighbour(mobility, -2, -1))
    diagonal = weight_sum(weights)
    mobility_coarse = restrict(mobility)
    coarse_weights = scaled_weights(face_weights(mobility_coarse, neighbour(mobility_coarse, -2, 1), neighbour(mobility_coarse, -2, -1)))
    coarse_diagonal = weight_sum(coarse_weights)

    def slice_end(initial):
        return fine_step(initial, mobility, weights, diagonal, coarse_weights, coarse_diagonal)

    ends = lax.map(slice_end, start_states)

    def advance(carried, paired):
        initial, ending = paired
        coarse_end = restrict(ending)
        following = coarse_step(carried, mobility_coarse) + (coarse_end - coarse_step(restrict(initial), mobility_coarse))
        return following, ending + prolong(following - coarse_end)

    unused, next_states = lax.scan(advance, restrict(start_states[0]), (start_states, ends))
    return next_states
```

```python
import jax
import jax.numpy as jnp
from jax import lax
from jax.experimental import pallas as pl
from jax.experimental.pallas import tpu as pltpu
from jax.sharding import Mesh, PartitionSpec as P

F32 = jnp.float32
HIGH = lax.Precision.HIGHEST
VM = pl.BlockSpec(memory_space=pltpu.VMEM)
SM = pl.BlockSpec(memory_space=pltpu.SMEM)

NXB = 16
HS = 11
HP = 10
WN = NXB + 2 * HP
CN = WN // 2


def shape(*dims):
    return jax.ShapeDtypeStruct(dims, F32)


def call(kernel, outs, ins, scratch=(), flops=1000000):
    specs = [SM if a.dtype == jnp.int32 and a.ndim == 1 else VM for a in ins]
    moved = sum(a.size * 4 for a in ins) + sum(4 * _size(o) for o in outs)
    return pl.pallas_call(
        kernel,
        out_shape=outs,
        in_specs=specs,
        out_specs=[VM] * len(outs),
        scratch_shapes=list(scratch),
        compiler_params=pltpu.CompilerParams(vmem_limit_bytes=28 * 1024 * 1024),
        cost_estimate=pl.CostEstimate(flops=flops, bytes_accessed=moved, transcendentals=0),
    )(*ins)


def _size(o):
    n = 1
    for d in o.shape:
        n *= d
    return n


def loop(lo, hi, fn, unroll=2):
    assert (hi - lo) % unroll == 0

    def step(t, carry):
        for u in range(unroll):
            fn(lo + t * unroll + u)
        return carry

    lax.fori_loop(0, (hi - lo) // unroll, step, 0)


def iota(dim):
    return lax.broadcasted_iota(jnp.int32, (8, 128), dim)


def quad(ref, *at):
    return [[ref[(*at, zp, slice(None), slice(128 * yp, 128 * yp + 128))] for yp in (0, 1)] for zp in (0, 1)]


def put(ref, at, zp, yp, value):
    ref[(*at, zp, slice(None), slice(128 * yp, 128 * yp + 128))] = value


def z_up(v, fix=None):
    f = fix or (lambda r: r)
    return [v[1], [f(pltpu.roll(v[0][q], 7, 0)) for q in (0, 1)]]


def z_down(v, fix=None):
    f = fix or (lambda r: r)
    return [[f(pltpu.roll(v[1][q], 1, 0)) for q in (0, 1)], v[0]]


def y_up(v, fix=None):
    f = fix or (lambda r: r)
    return [[v[q][1], f(pltpu.roll(v[q][0], 127, 1))] for q in (0, 1)]


def y_down(v, fix=None):
    f = fix or (lambda r: r)
    return [[f(pltpu.roll(v[q][1], 1, 1)), v[q][0]] for q in (0, 1)]


class Fix:
    def __init__(self):
        k, j = iota(0), iota(1)
        self.zu = lambda r: jnp.where(k < 7, r, 0.0)
        self.zd = lambda r: jnp.where(k > 0, r, 0.0)
        self.yu = lambda r: jnp.where(j < 127, r, 0.0)
        self.yd = lambda r: jnp.where(j > 0, r, 0.0)


def coarse_near(v, fix):
    return (
        fix.zu(pltpu.roll(v, 7, 0)),
        fix.zd(pltpu.roll(v, 1, 0)),
        fix.yu(pltpu.roll(v, 127, 1)),
        fix.yd(pltpu.roll(v, 1, 1)),
    )


def near(v, fix):
    return (z_up(v, fix.zu), z_down(v, fix.zd), y_up(v, fix.yu), y_down(v, fix.yd))


def raw_near(v):
    return (z_up(v), z_down(v), y_up(v), y_down(v))


QUAD = [(zp, yp) for zp in (0, 1) for yp in (0, 1)]


def eight(ref, i):
    total = None
    for layer in (i, i + 1):
        v = quad(ref, layer)
        for zp, yp in QUAD:
            total = v[zp][yp] if total is None else total + v[zp][yp]
    return total


def split_matrix():
    r = lax.broadcasted_iota(jnp.int32, (256, 256), 0)
    c = lax.broadcasted_iota(jnp.int32, (256, 256), 1)
    return jnp.where(r == jnp.where(c < 128, 2 * c, 2 * c - 255), 1.0, 0.0).astype(F32)


def join_matrix():
    r = lax.broadcasted_iota(jnp.int32, (256, 256), 0)
    c = lax.broadcasted_iota(jnp.int32, (256, 256), 1)
    return jnp.where(c == jnp.where(r < 128, 2 * r, 2 * r - 255), 1.0, 0.0).astype(F32)


def rows_of(x, zp):
    return pl.ds(zp * NXB + x, 8, stride=2 * NXB)


def prepare(info, start, labels, s_out, m_out, outer, inner, rows):
    core = info[0]
    split = split_matrix()
    for c in range(4):
        for x in range(NXB):
            for zp in (0, 1):
                to = pl.ds((x * 2 + zp) * 8, 8)
                for q in (0, 1):
                    cols = slice(128 * q, 128 * q + 128)
                    if c < 3:
                        rows[to, cols] = start[c * 2 + q, rows_of(x, zp), :]
                    else:
                        rows[to, cols] = 1.0 / (1.0 + 3.0 * labels[q, rows_of(x, zp), :].astype(F32))
        done = jnp.dot(rows[...], split, precision=HIGH, preferred_element_type=F32)
        done = done.reshape(NXB, 2, 8, 256)
        if c < 3:
            s_out[c] = done
        else:
            m_out[...] = done
    for c in range(3):
        outer[pl.ds(c * HS, HS)] = s_out[c, pl.ds((NXB - HS) * core, HS)]
        inner[pl.ds(c * HS, HS)] = s_out[c, pl.ds((NXB - HS) * (1 - core), HS)]
    outer[pl.ds(3 * HS, HP)] = m_out[pl.ds((NXB - HP) * core, HP)]
    inner[pl.ds(3 * HS, HP)] = m_out[pl.ds((NXB - HP) * (1 - core), HP)]


def interleave(base, nat):
    join = join_matrix()
    for c in range(3):
        done = jnp.dot(base[c].reshape(256, 256), join, precision=HIGH, preferred_element_type=F32)
        for x in range(NXB):
            for zp in (0, 1):
                at = (x * 2 + zp) * 8
                for q in (0, 1):
                    nat[c * 2 + q, rows_of(x, zp), :] = done[at : at + 8, 128 * q : 128 * q + 128]


def finish(nat, w, out):
    r = lax.broadcasted_iota(jnp.int32, (128, 256), 0)
    c = lax.broadcasted_iota(jnp.int32, (128, 256), 1)
    spread = jnp.where(lax.div(c, 2) == r, 1.0, 0.0).astype(F32)
    done = jnp.dot(w[...].reshape(192, 128), spread, precision=HIGH, preferred_element_type=F32)
    for comp in range(3):
        for xc in range(NXB // 2):
            at = (comp * 8 + xc) * 8
            for q in (0, 1):
                value = done[at : at + 8, 128 * q : 128 * q + 128]
                for xp in (0, 1):
                    for zp in (0, 1):
                        sl = rows_of(2 * xc + xp, zp)
                        out[comp * 2 + q, sl, :] = nat[comp * 2 + q, sl, :] + value


def valid_of(info):
    left, right = info[1].astype(F32), info[2].astype(F32)
    return lambda i, halo: jnp.where(i < halo, left, jnp.where(i >= halo + NXB, right, 1.0))


def weigh(valid, mw, wt, dg, inv, mc, cw, cinv, fix):
    def layer(i):
        m = quad(mw, i)
        sides = near(m, fix) + (quad(mw, i + 1), quad(mw, i - 1))
        ok = valid(i, HP)
        for zp, yp in QUAD:
            faces = [0.5 * (m[zp][yp] + s[zp][yp]) for s in sides]
            total = faces[0] + faces[1] + faces[2] + faces[3] + faces[4] + faces[5]
            if zp == 1:
                faces[0] = fix.zu(faces[0])
            else:
                faces[1] = fix.zd(faces[1])
            if yp == 1:
                faces[2] = fix.yu(faces[2])
            else:
                faces[3] = fix.yd(faces[3])
            for f in range(6):
                put(wt, (f, i), zp, yp, faces[f])
            put(dg, (i,), zp, yp, total)
            put(inv, (i,), zp, yp, (0.8 * ok) / (total + (1.0 - ok)))

    loop(1, WN - 1, layer)

    def coarse(j):
        mc[j] = 0.125 * eight(mw, 2 * j)

    loop(0, CN, coarse)

    def coarse_layer(j):
        m = mc[j]
        sides = coarse_near(m, fix) + (mc[j + 1], mc[j - 1])
        ok = valid(2 * j, HP)
        faces = [0.125 * (m + s) for s in sides]
        total = faces[0] + faces[1] + faces[2] + faces[3] + faces[4] + faces[5]
        faces[0] = fix.zu(faces[0])
        faces[1] = fix.zd(faces[1])
        faces[2] = fix.yu(faces[2])
        faces[3] = fix.yd(faces[3])
        for f in range(6):
            cw[f, j] = faces[f]
        cinv[j] = (0.8 * ok) / (total + (1.0 - ok))

    loop(1, CN - 1, coarse_layer)


def gathered(p, i, wt):
    v = quad(p, i)
    sides = raw_near(v) + (quad(p, i + 1), quad(p, i - 1))
    ws = [quad(wt, f, i) for f in range(6)]
    total = [[None, None], [None, None]]
    for zp, yp in QUAD:
        terms = [ws[f][zp][yp] * sides[f][zp][yp] for f in range(6)]
        total[zp][yp] = ((terms[0] + terms[1]) + (terms[2] + terms[3])) + (terms[4] + terms[5])
    return v, total


def smooth(lo, hi, p, q, tw, wt, inv, unroll=2):
    def layer(i):
        v, total = gathered(p, i, wt)
        t, n = quad(tw, i), quad(inv, i)
        for zp, yp in QUAD:
            put(q, (i,), zp, yp, 0.2 * v[zp][yp] + n[zp][yp] * (t[zp][yp] + total[zp][yp]))

    loop(lo, hi, layer, unroll)


def correct(p, tw, wt, dg, lo, ca, cb, cw, cinv):
    def coarse(j):
        out = None
        for i in (2 * j, 2 * j + 1):
            v, total = gathered(p, i, wt)
            t, d = quad(tw, i), quad(dg, i)
            for zp, yp in QUAD:
                r = (t[zp][yp] + total[zp][yp]) - d[zp][yp] * v[zp][yp]
                out = r if out is None else out + r
        out = 0.125 * out
        lo[j] = out
        ca[j] = cinv[j] * out

    loop(1, CN - 1, coarse, 1)

    def sweep(first, last, a, b):
        def layer(j):
            v = a[j]
            sides = (
                pltpu.roll(v, 7, 0),
                pltpu.roll(v, 1, 0),
                pltpu.roll(v, 127, 1),
                pltpu.roll(v, 1, 1),
                a[j + 1],
                a[j - 1],
            )
            terms = [cw[f, j] * sides[f] for f in range(6)]
            total = ((terms[0] + terms[1]) + (terms[2] + terms[3])) + (terms[4] + terms[5])
            b[j] = 0.2 * v + cinv[j] * (lo[j] + total)

        loop(first, last, layer)

    sweep(2, CN - 2, ca, cb)
    sweep(3, CN - 3, cb, ca)
    sweep(4, CN - 4, ca, cb)

    def add(j):
        g = cb[j]
        for i in (2 * j, 2 * j + 1):
            v = quad(p, i)
            for zp, yp in QUAD:
                put(p, (i,), zp, yp, v[zp][yp] + g)

    loop(4, CN - 4, add)


def first_cycle(info, s_own, m_own, off, on, pred, tw, mw, p1, outer, inner, gs, sw, wt, dg, inv, pr, p, mc, cw, cinv, lo, ca, cb, rs, rt):
    fix = Fix()
    core = info[0]
    valid = valid_of(info)
    off_s, on_s = core * (HS + NXB), (1 - core) * (HS + NXB)
    off_m, on_m = core * (HP + NXB), (1 - core) * (HP + NXB)
    for c in range(3):
        sw[c, pl.ds(HS, NXB)] = s_own[c]
        sw[c, pl.ds(off_s, HS)] = off[pl.ds(c * HS, HS)]
        sw[c, pl.ds(on_s, HS)] = on[pl.ds(c * HS, HS)]
    mw[pl.ds(HP, NXB)] = m_own[...]
    mw[pl.ds(off_m, HP)] = off[pl.ds(3 * HS, HP)]
    mw[pl.ds(on_m, HP)] = on[pl.ds(3 * HS, HP)]
    weigh(valid, mw, wt, dg, inv, mc, cw, cinv, fix)

    def predict(i):
        ok = valid(i, HP)
        m = quad(mw, i)
        for c in range(3):
            v = quad(sw, c, i + 1)
            sides = near(v, fix) + (quad(sw, c, i + 2), quad(sw, c, i))
            for zp, yp in QUAD:
                n = [s[zp][yp] for s in sides]
                total = ((n[0] + n[1]) + (n[2] + n[3])) + (n[4] + n[5])
                value = 0.4 * v[zp][yp] + 0.1 * total
                if c == 0:
                    value = value + (0.4 * m[zp][yp] - 0.2)
                put(pr, (c, i), zp, yp, ok * value)

    loop(0, WN, predict, 1)

    def aim(i):
        a, b = quad(pr, 0, i), quad(pr, 2, i)
        zu, zd = z_up(a, fix.zu), z_down(a, fix.zd)
        yu, yd = y_up(b, fix.yu), y_down(b, fix.yd)
        xu, xd = quad(pr, 1, i + 1), quad(pr, 1, i - 1)
        n = quad(inv, i)
        for zp, yp in QUAD:
            t = (zu[zp][yp] - zd[zp][yp]) + (xu[zp][yp] - xd[zp][yp])
            t = -0.5 * (t + (yu[zp][yp] - yd[zp][yp]))
            put(tw, (i,), zp, yp, t)
            put(p, (i,), zp, yp, n[zp][yp] * t)

    loop(1, WN - 1, aim)
    for c in range(3):
        pred[c] = pr[c, pl.ds(HP, NXB)]

    correct(p, tw, wt, dg, lo, ca, cb, cw, cinv)

    def last(x):
        i = x + HP
        v, total = gathered(p, i, wt)
        t, n = quad(tw, i), quad(inv, i)
        for zp, yp in QUAD:
            put(p1, (x,), zp, yp, 0.2 * v[zp][yp] + n[zp][yp] * (t[zp][yp] + total[zp][yp]))

    loop(0, NXB, last)
    outer[...] = p1[pl.ds((NXB - HP) * core, HP)]
    inner[...] = p1[pl.ds((NXB - HP) * (1 - core), HP)]

    later = info[3].astype(F32)

    def shrink(q):
        for c in range(3):
            rs[c, q] = 0.125 * eight(sw.at[c], 2 * q + 7)

    loop(0, 12, shrink, 1)

    def coarse_step(a, b, scale):
        def layer(q):
            m = mc[q + 3]
            for c in range(3):
                v = a[c, q]
                n = coarse_near(v, fix) + (a[c, q + 1], a[c, q - 1])
                total = ((n[0] + n[1]) + (n[2] + n[3])) + (n[4] + n[5])
                b(c, q, scale * ((1.0 - 0.9 * m) * v + (0.15 * m) * total))

        return layer

    def to_rt(c, q, value):
        rt[c, q] = value

    def to_gs(c, q, value):
        gs[c, q - 2] = value

    loop(1, 11, coarse_step(rs, to_rt, 1.0), 1)
    loop(2, 10, coarse_step(rt, to_gs, later), 1)


def second_cycle(info, pred, tw, mw, p1, off, on, gs, base, send, wt, dg, inv, p, q, mc, cw, cinv, lo, ca, cb):
    fix = Fix()
    core, row = info[0], info[4]
    valid = valid_of(info)
    p[pl.ds(HP, NXB)] = p1[...]
    p[pl.ds(core * (HP + NXB), HP)] = off[...]
    p[pl.ds((1 - core) * (HP + NXB), HP)] = on[...]
    weigh(valid, mw, wt, dg, inv, mc, cw, cinv, fix)
    smooth(1, WN - 1, p, q, tw, wt, inv)
    correct(q, tw, wt, dg, lo, ca, cb, cw, cinv)
    smooth(HP - 1, HP + NXB + 1, q, p, tw, wt, inv)

    def finish_pair(j):
        sums = [None, None, None]
        held = []
        for i in (2 * j, 2 * j + 1):
            v = quad(p, i + HP)
            sides = near(v, fix)
            xu, xd = quad(p, i + HP + 1), quad(p, i + HP - 1)
            m = quad(mw, i + HP)
            up = (sides[0], xu, sides[2])
            down = (sides[1], xd, sides[3])
            for c in range(3):
                a = quad(pred, c, i)
                for zp, yp in QUAD:
                    e = a[zp][yp] - (0.5 * m[zp][yp]) * (up[c][zp][yp] - down[c][zp][yp])
                    held.append((c, i, zp, yp, e))
                    sums[c] = e if sums[c] is None else sums[c] + e
        means = [0.125 * s for s in sums]
        for c, i, zp, yp, e in held:
            put(base, (c, i), zp, yp, e - means[c])
        for c in range(3):
            r = means[c] - gs[c, j]
            for to in range(4):
                send[to, c, lax.div(j, 4), lax.rem(j, 4)] = r
                if c == 0:
                    send[to, 3, lax.div(j, 4), lax.rem(j, 4)] = jnp.zeros_like(r)

    loop(0, NXB // 2, finish_pair, 1)
    for half in (0, 1):
        g = mc[HP // 2 + 4 * half + row]
        for to in range(4):
            for chip in range(4):
                send[to, chip, half, 4] = g


NC = 64


def substep(a, b, wa, wb, fix):
    for i in range(NC):
        v = a[i]
        n = coarse_near(v, fix)
        total = (n[0] + n[1]) + (n[2] + n[3])
        if i > 0:
            total = total + a[i - 1]
        if i < NC - 1:
            total = total + a[i + 1]
        b[i] = wa[i] * v + wb[i] * total


def advance(times, a, b, wa, wb, fix):
    def turn(t, carry):
        substep(a, b, wa, wb, fix)
        substep(b, a, wa, wb, fix)
        return carry

    lax.fori_loop(0, times, turn, 0)


def rows_scan(info, got, swapped, acc, half, wa, wb, b):
    fix = Fix()
    core, row = info[0], info[4]
    for s in range(8):
        for l in range(4):
            for at, src in ((8 * s + 4 * core + l, got), (8 * s + 4 * (1 - core) + l, swapped)):
                m = src[l, s, 4]
                wa[at] = 1.0 - 0.9 * m
                wb[at] = 0.15 * m
                acc[at] = src[0, s, l]
    for t in range(1, 4):

        @pl.when(t <= row)
        def _():
            advance(8, acc, b, wa, wb, fix)
            for s in range(8):
                for l in range(4):
                    own, other = 8 * s + 4 * core + l, 8 * s + 4 * (1 - core) + l
                    acc[own] = acc[own] + got[t, s, l]
                    acc[other] = acc[other] + swapped[t, s, l]

    half[...] = acc[pl.ds(NC // 2 * core, NC // 2)]


def shift_scan(times, last):
    def kernel(info, acc, own, other, wa, wb, *rest):
        if last:
            half, a, b = rest
            out = a
        else:
            out, half, a, b = rest
        fix = Fix()
        core = info[0]
        a[pl.ds(NC // 2 * core, NC // 2)] = own[...]
        a[pl.ds(NC // 2 * (1 - core), NC // 2)] = other[...]
        advance(times, a, b, wa, wb, fix)
        for i in range(NC):
            out[i] = acc[i] + a[i]
        if last:
            for s in range(8):
                half[s] = out[pl.ds(8 * s + 4 * core, 4)]
        else:
            half[...] = out[pl.ds(NC // 2 * core, NC // 2)]

    return kernel


def body(ny, nz, start_states, labels):
    ns = lax.axis_size("space")
    s = lax.axis_index("space")
    y = lax.axis_index("y")
    z = lax.axis_index("z")
    core = lax.rem(s, 2)
    info = jnp.stack([core, s > 0, s < ns - 1, y * nz + z > 0, y, s, s, s]).astype(jnp.int32)
    swap = [(i, i ^ 1) for i in range(ns)]
    cross = [(i, i + 1) for i in range(1, ns - 1, 2)]
    cross = cross + [(b, a) for a, b in cross]

    def exchange(outer, inner):
        off = lax.ppermute(outer, "space", cross)
        on = lax.ppermute(inner, "space", swap)
        return off, on

    start = start_states[0].reshape(3, 256, 2, 128).transpose(0, 2, 1, 3).reshape(6, 256, 128)
    label = labels.reshape(256, 2, 128).transpose(1, 0, 2)
    layer = (2, 8, 256)
    edge = 3 * HS + HP
    vm = lambda *d: pltpu.VMEM(d, F32)
    s_own, m_own, outer, inner = call(
        prepare,
        [shape(3, NXB, *layer), shape(NXB, *layer), shape(edge, *layer), shape(edge, *layer)],
        [info, start, label],
        [vm(256, 256)],
    )
    off, on = exchange(outer, inner)
    coarse = [vm(CN, 8, 128), vm(6, CN, 8, 128), vm(CN, 8, 128), vm(CN, 8, 128), vm(CN, 8, 128), vm(CN, 8, 128)]
    fine = [vm(6, WN, *layer), vm(WN, *layer), vm(WN, *layer)]
    pred, tw, mw, p1, outer, inner, gs = call(
        first_cycle,
        [
            shape(3, NXB, *layer),
            shape(WN, *layer),
            shape(WN, *layer),
            shape(NXB, *layer),
            shape(HP, *layer),
            shape(HP, *layer),
            shape(3, 8, 8, 128),
        ],
        [info, s_own, m_own, off, on],
        [vm(3, NXB + 2 * HS, *layer)] + fine + [vm(3, WN, *layer), vm(WN, *layer)] + coarse + [vm(3, 12, 8, 128)] * 2,
    )
    off, on = exchange(outer, inner)
    base, send = call(
        second_cycle,
        [shape(3, NXB, *layer), shape(4, 4, 2, 5, 8, 128)],
        [info, pred, tw, mw, p1, off, on, gs],
        fine + [vm(WN, *layer), vm(WN, *layer)] + coarse,
    )
    got = lax.all_to_all(send.reshape(ny * ns, 5, 8, 128), ("y", "space"), 0, 0)
    got = got.reshape(ny, ns, 5, 8, 128)
    swapped = lax.ppermute(got, "space", swap)
    acc, half, wa, wb = call(
        rows_scan,
        [shape(NC, 8, 128), shape(NC // 2, 8, 128), shape(NC, 8, 128), shape(NC, 8, 128)],
        [info, got, swapped],
        [vm(NC, 8, 128)],
    )
    nt = ny * nz
    for k in (1, 2, 4):
        own = lax.ppermute(half, ("y", "z"), [(i, i + k) for i in range(nt - k)])
        other = lax.ppermute(own, "space", swap)
        last = k == 4
        outs = [shape(8, 4, 8, 128)] if last else [shape(NC, 8, 128), shape(NC // 2, 8, 128)]
        done = call(shift_scan(k, last), outs, [info, acc, own, other, wa, wb], [vm(NC, 8, 128)] * 2)
        if last:
            chunks = done[0]
        else:
            acc, half = done
    (nat,) = call(interleave, [shape(6, 256, 128)], [base])
    back = lax.all_to_all(chunks, "space", 0, 0)
    w = back[:6].reshape(3, 8, 8, 128)
    (out,) = call(finish, [shape(6, 256, 128)], [nat, w])
    out = out.reshape(3, 2, 256, 128).transpose(0, 2, 1, 3)
    return out.reshape(1, 3, 16, NXB, 256)


def solution(mesh):
    nz = 8
    ny = mesh.shape["tm"] // nz
    split = Mesh(mesh.devices.reshape(ny, nz, mesh.shape["space"]), ("y", "z", "space"))
    in_specs = (P(("y", "z"), None, None, "space", None), P(None, "space", None))
    out_specs = P(("y", "z"), None, None, "space", None)

    def run(start_states, labels):
        return body(ny, nz, start_states, labels)

    return jax.shard_map(run, mesh=split, in_specs=in_specs, out_specs=out_specs, check_vma=False)
```

```python
import jax
import jax.numpy as jnp
from jax import lax
from jax.experimental import pallas as pl
from jax.experimental.pallas import tpu as pltpu
from jax.sharding import Mesh, PartitionSpec as P

F32 = jnp.float32
HIGH = lax.Precision.HIGHEST
VM = pl.BlockSpec(memory_space=pltpu.VMEM)
SM = pl.BlockSpec(memory_space=pltpu.SMEM)
ANY = pl.BlockSpec(memory_space=pltpu.HBM)

NXB = 16
HS = 11
HP = 10
WN = NXB + 2 * HP
CN = WN // 2


def shape(*dims):
    return jax.ShapeDtypeStruct(dims, F32)


def call(kernel, outs, ins, scratch=(), where=VM):
    specs = [SM if a.dtype == jnp.int32 and a.ndim == 1 else where for a in ins]
    moved = sum(a.size * 4 for a in ins) + sum(4 * _size(o) for o in outs)
    return pl.pallas_call(
        kernel,
        out_shape=outs,
        in_specs=specs,
        out_specs=[VM] * len(outs),
        scratch_shapes=list(scratch),
        compiler_params=pltpu.CompilerParams(vmem_limit_bytes=28 * 1024 * 1024),
        cost_estimate=pl.CostEstimate(flops=1000000, bytes_accessed=moved, transcendentals=0),
    )(*ins)


def _size(o):
    n = 1
    for d in o.shape:
        n *= d
    return n


def loop(lo, hi, fn, unroll=0):
    unroll = unroll or hi - lo
    if unroll == hi - lo:
        for i in range(lo, hi):
            fn(i)
        return
    assert (hi - lo) % unroll == 0

    def step(t, carry):
        for u in range(unroll):
            fn(lo + t * unroll + u)
        return carry

    lax.fori_loop(0, (hi - lo) // unroll, step, 0)


def iota(dim):
    return lax.broadcasted_iota(jnp.int32, (8, 128), dim)


def quad(ref, *at):
    return [[ref[(*at, zp, slice(None), slice(128 * yp, 128 * yp + 128))] for yp in (0, 1)] for zp in (0, 1)]


def put(ref, at, zp, yp, value):
    ref[(*at, zp, slice(None), slice(128 * yp, 128 * yp + 128))] = value


def z_up(v, fix=None):
    f = fix or (lambda r: r)
    return [v[1], [f(pltpu.roll(v[0][q], 7, 0)) for q in (0, 1)]]


def z_down(v, fix=None):
    f = fix or (lambda r: r)
    return [[f(pltpu.roll(v[1][q], 1, 0)) for q in (0, 1)], v[0]]


def y_up(v, fix=None):
    f = fix or (lambda r: r)
    return [[v[q][1], f(pltpu.roll(v[q][0], 127, 1))] for q in (0, 1)]


def y_down(v, fix=None):
    f = fix or (lambda r: r)
    return [[f(pltpu.roll(v[q][1], 1, 1)), v[q][0]] for q in (0, 1)]


class Fix:
    def __init__(self):
        k, j = iota(0), iota(1)
        self.zu = lambda r: jnp.where(k < 7, r, 0.0)
        self.zd = lambda r: jnp.where(k > 0, r, 0.0)
        self.yu = lambda r: jnp.where(j < 127, r, 0.0)
        self.yd = lambda r: jnp.where(j > 0, r, 0.0)


def coarse_near(v, fix):
    return (
        fix.zu(pltpu.roll(v, 7, 0)),
        fix.zd(pltpu.roll(v, 1, 0)),
        fix.yu(pltpu.roll(v, 127, 1)),
        fix.yd(pltpu.roll(v, 1, 1)),
    )


def near(v, fix):
    return (z_up(v, fix.zu), z_down(v, fix.zd), y_up(v, fix.yu), y_down(v, fix.yd))


def raw_near(v):
    return (z_up(v), z_down(v), y_up(v), y_down(v))


QUAD = [(zp, yp) for zp in (0, 1) for yp in (0, 1)]


def eight(ref, i):
    total = None
    for layer in (i, i + 1):
        v = quad(ref, layer)
        for zp, yp in QUAD:
            total = v[zp][yp] if total is None else total + v[zp][yp]
    return total


def split_matrix():
    r = lax.broadcasted_iota(jnp.int32, (256, 256), 0)
    c = lax.broadcasted_iota(jnp.int32, (256, 256), 1)
    return jnp.where(r == jnp.where(c < 128, 2 * c, 2 * c - 255), 1.0, 0.0).astype(F32)


def join_matrix():
    r = lax.broadcasted_iota(jnp.int32, (256, 256), 0)
    c = lax.broadcasted_iota(jnp.int32, (256, 256), 1)
    return jnp.where(c == jnp.where(r < 128, 2 * r, 2 * r - 255), 1.0, 0.0).astype(F32)


def parity_matrix():
    r = lax.broadcasted_iota(jnp.int32, (128, 128), 0)
    c = lax.broadcasted_iota(jnp.int32, (128, 128), 1)
    return jnp.where(r == jnp.where(c < 64, 2 * c, 2 * c - 127), 1.0, 0.0).astype(F32)


def rows_of(x, zp, q):
    return pl.ds((4 * zp + 2 * (x // 8) + q) * 8 + x % 8, 8, stride=64)


def prepare(info, start, labels, s_out, m_out, outer, inner, s_in, l_in, rows, sems):
    core = info[0]
    copies = [pltpu.make_async_copy(labels, l_in, sems.at[3])]
    copies += [pltpu.make_async_copy(start.at[c], s_in.at[c], sems.at[c]) for c in range(3)]
    for copy in copies:
        copy.start()
    split = split_matrix()
    copies[0].wait()
    for x in range(NXB):
        for zp in (0, 1):
            for q in (0, 1):
                mobility = 1.0 / (1.0 + 3.0 * l_in[rows_of(x, zp, q), :].astype(F32))
                rows[3, pl.ds((x * 2 + zp) * 8, 8), 128 * q : 128 * q + 128] = mobility
    done = jnp.dot(rows[3], split, precision=HIGH, preferred_element_type=F32)
    m_out[...] = done.reshape(NXB, 2, 8, 256)
    outer[pl.ds(3 * HS, HP)] = m_out[pl.ds((NXB - HP) * core, HP)]
    inner[pl.ds(3 * HS, HP)] = m_out[pl.ds((NXB - HP) * (1 - core), HP)]
    for c in range(3):
        copies[1 + c].wait()
        for x in range(NXB):
            for zp in (0, 1):
                for q in (0, 1):
                    rows[c, pl.ds((x * 2 + zp) * 8, 8), 128 * q : 128 * q + 128] = s_in[c, rows_of(x, zp, q), :]
        done = jnp.dot(rows[c], split, precision=HIGH, preferred_element_type=F32)
        s_out[c] = done.reshape(NXB, 2, 8, 256)
        outer[pl.ds(c * HS, HS)] = s_out[c, pl.ds((NXB - HS) * core, HS)]
        inner[pl.ds(c * HS, HS)] = s_out[c, pl.ds((NXB - HS) * (1 - core), HS)]


def interleave(base, nat):
    join = join_matrix()
    for c in range(3):
        done = jnp.dot(base[c].reshape(256, 256), join, precision=HIGH, preferred_element_type=F32)
        for x in range(NXB):
            for zp in (0, 1):
                at = (x * 2 + zp) * 8
                for q in (0, 1):
                    cols = slice(128 * q, 128 * q + 128)
                    nat[c, rows_of(x, zp, q), :] = done[at : at + 8, cols]


def finish(nat, w, out):
    r = lax.broadcasted_iota(jnp.int32, (128, 256), 0)
    c = lax.broadcasted_iota(jnp.int32, (128, 256), 1)
    spread = jnp.where(lax.div(c, 2) == jnp.where(r < 64, 2 * r, 2 * r - 127), 1.0, 0.0).astype(F32)
    done = jnp.dot(w[...].reshape(192, 128), spread, precision=HIGH, preferred_element_type=F32)
    for comp in range(3):
        for xc in range(NXB // 2):
            at = (comp * 8 + xc) * 8
            for q in (0, 1):
                cols = slice(128 * q, 128 * q + 128)
                value = done[at : at + 8, cols]
                for xp in (0, 1):
                    for zp in (0, 1):
                        sl = rows_of(2 * xc + xp, zp, q)
                        out[comp, sl, :] = nat[comp, sl, :] + value


def valid_of(info):
    left, right = info[1].astype(F32), info[2].astype(F32)
    return lambda i, halo: jnp.where(i < halo, left, jnp.where(i >= halo + NXB, right, jnp.float32(1.0)))


def weigh(valid, mw, wt, dg, inv, mc, cw, cinv, fix):
    def layer(i):
        m = quad(mw, i)
        sides = near(m, fix) + (quad(mw, i + 1), quad(mw, i - 1))
        ok = valid(i, HP)
        for zp, yp in QUAD:
            faces = [0.5 * (m[zp][yp] + s[zp][yp]) for s in sides]
            total = faces[0] + faces[1] + faces[2] + faces[3] + faces[4] + faces[5]
            if zp == 1:
                faces[0] = fix.zu(faces[0])
            else:
                faces[1] = fix.zd(faces[1])
            if yp == 1:
                faces[2] = fix.yu(faces[2])
            else:
                faces[3] = fix.yd(faces[3])
            for f in range(6):
                put(wt, (f, i), zp, yp, faces[f])
            put(dg, (i,), zp, yp, total)
            put(inv, (i,), zp, yp, (0.8 * ok) / (total + (1.0 - ok)))

    loop(1, WN - 1, layer, 17)

    def coarse(j):
        mc[j] = 0.125 * eight(mw, 2 * j)

    loop(0, CN, coarse)

    def coarse_layer(j):
        m = mc[j]
        sides = coarse_near(m, fix) + (mc[j + 1], mc[j - 1])
        ok = valid(2 * j, HP)
        faces = [0.125 * (m + s) for s in sides]
        total = faces[0] + faces[1] + faces[2] + faces[3] + faces[4] + faces[5]
        faces[0] = fix.zu(faces[0])
        faces[1] = fix.zd(faces[1])
        faces[2] = fix.yu(faces[2])
        faces[3] = fix.yd(faces[3])
        for f in range(6):
            cw[f, j] = faces[f]
        cinv[j] = (0.8 * ok) / (total + (1.0 - ok))

    loop(1, CN - 1, coarse_layer)


def gathered(p, i, wt):
    v = quad(p, i)
    sides = raw_near(v) + (quad(p, i + 1), quad(p, i - 1))
    ws = [quad(wt, f, i) for f in range(6)]
    total = [[None, None], [None, None]]
    for zp, yp in QUAD:
        terms = [ws[f][zp][yp] * sides[f][zp][yp] for f in range(6)]
        total[zp][yp] = ((terms[0] + terms[1]) + (terms[2] + terms[3])) + (terms[4] + terms[5])
    return v, total


def smooth(lo, hi, p, q, tw, wt, inv):
    def layer(i):
        v, total = gathered(p, i, wt)
        t, n = quad(tw, i), quad(inv, i)
        for zp, yp in QUAD:
            put(q, (i,), zp, yp, 0.2 * v[zp][yp] + n[zp][yp] * (t[zp][yp] + total[zp][yp]))

    loop(lo, hi, layer, (hi - lo) // 2)


def correct(p, tw, wt, dg, lo, ca, cb, cw, cinv):
    def coarse(j):
        out = None
        for i in (2 * j, 2 * j + 1):
            v, total = gathered(p, i, wt)
            t, d = quad(tw, i), quad(dg, i)
            for zp, yp in QUAD:
                r = (t[zp][yp] + total[zp][yp]) - d[zp][yp] * v[zp][yp]
                out = r if out is None else out + r
        out = 0.125 * out
        lo[j] = out
        ca[j] = cinv[j] * out

    loop(1, CN - 1, coarse, 8)

    def sweep(first, last, a, b):
        def layer(j):
            v = a[j]
            sides = (
                pltpu.roll(v, 7, 0),
                pltpu.roll(v, 1, 0),
                pltpu.roll(v, 127, 1),
                pltpu.roll(v, 1, 1),
                a[j + 1],
                a[j - 1],
            )
            terms = [cw[f, j] * sides[f] for f in range(6)]
            total = ((terms[0] + terms[1]) + (terms[2] + terms[3])) + (terms[4] + terms[5])
            b[j] = 0.2 * v + cinv[j] * (lo[j] + total)

        loop(first, last, layer)

    sweep(2, CN - 2, ca, cb)
    sweep(3, CN - 3, cb, ca)
    sweep(4, CN - 4, ca, cb)

    def add(j):
        g = cb[j]
        for i in (2 * j, 2 * j + 1):
            v = quad(p, i)
            for zp, yp in QUAD:
                put(p, (i,), zp, yp, v[zp][yp] + g)

    loop(4, CN - 4, add)


def weights(info, m_own, off, on, mw, wt, dg, inv, mc, cw, cinv):
    core = info[0]
    mw[pl.ds(HP, NXB)] = m_own[...]
    mw[pl.ds(core * (HP + NXB), HP)] = off[pl.ds(3 * HS, HP)]
    mw[pl.ds((1 - core) * (HP + NXB), HP)] = on[pl.ds(3 * HS, HP)]
    weigh(valid_of(info), mw, wt, dg, inv, mc, cw, cinv, Fix())


def first_cycle(info, s_own, off, on, mw, wt, dg, inv, mc, cw, cinv, pred, tw, p1, outer, inner, gs, sw, pr, p, lo, ca, cb, rs, rt):
    fix = Fix()
    core = info[0]
    valid = valid_of(info)
    off_s, on_s = core * (HS + NXB), (1 - core) * (HS + NXB)
    for c in range(3):
        sw[c, pl.ds(HS, NXB)] = s_own[c]
        sw[c, pl.ds(off_s, HS)] = off[pl.ds(c * HS, HS)]
        sw[c, pl.ds(on_s, HS)] = on[pl.ds(c * HS, HS)]

    def predict(i):
        ok = valid(i, HP)
        m = quad(mw, i)
        for c in range(3):
            v = quad(sw, c, i + 1)
            sides = near(v, fix) + (quad(sw, c, i + 2), quad(sw, c, i))
            for zp, yp in QUAD:
                n = [s[zp][yp] for s in sides]
                total = ((n[0] + n[1]) + (n[2] + n[3])) + (n[4] + n[5])
                value = 0.4 * v[zp][yp] + 0.1 * total
                if c == 0:
                    value = value + (0.4 * m[zp][yp] - 0.2)
                put(pr, (c, i), zp, yp, ok * value)

    loop(0, WN, predict, 6)

    def aim(i):
        a, b = quad(pr, 0, i), quad(pr, 2, i)
        zu, zd = z_up(a, fix.zu), z_down(a, fix.zd)
        yu, yd = y_up(b, fix.yu), y_down(b, fix.yd)
        xu, xd = quad(pr, 1, i + 1), quad(pr, 1, i - 1)
        n = quad(inv, i)
        for zp, yp in QUAD:
            t = (zu[zp][yp] - zd[zp][yp]) + (xu[zp][yp] - xd[zp][yp])
            t = -0.5 * (t + (yu[zp][yp] - yd[zp][yp]))
            put(tw, (i,), zp, yp, t)
            put(p, (i,), zp, yp, n[zp][yp] * t)

    loop(1, WN - 1, aim, 17)
    for c in range(3):
        pred[c] = pr[c, pl.ds(HP, NXB)]

    correct(p, tw, wt, dg, lo, ca, cb, cw, cinv)

    def last(x):
        i = x + HP
        v, total = gathered(p, i, wt)
        t, n = quad(tw, i), quad(inv, i)
        for zp, yp in QUAD:
            put(p1, (x,), zp, yp, 0.2 * v[zp][yp] + n[zp][yp] * (t[zp][yp] + total[zp][yp]))

    loop(0, NXB, last, 8)
    outer[...] = p1[pl.ds((NXB - HP) * core, HP)]
    inner[...] = p1[pl.ds((NXB - HP) * (1 - core), HP)]

    later = info[3].astype(F32)

    def shrink(q):
        for c in range(3):
            rs[c, q] = 0.125 * eight(sw.at[c], 2 * q + 7)

    loop(0, 12, shrink)

    def coarse_step(a, b, scale):
        def layer(q):
            m = mc[q + 3]
            for c in range(3):
                v = a[c, q]
                n = coarse_near(v, fix) + (a[c, q + 1], a[c, q - 1])
                total = ((n[0] + n[1]) + (n[2] + n[3])) + (n[4] + n[5])
                b(c, q, scale * ((1.0 - 0.9 * m) * v + (0.15 * m) * total))

        return layer

    def to_rt(c, q, value):
        rt[c, q] = value

    def to_gs(c, q, value):
        gs[c, q - 2] = value

    loop(1, 11, coarse_step(rs, to_rt, 1.0))
    loop(2, 10, coarse_step(rt, to_gs, later))


def second_cycle(info, pred, tw, p1, off, on, gs, mw, wt, dg, inv, mc, cw, cinv, base, send, p, q, lo, ca, cb, plain):
    fix = Fix()
    core, row = info[0], info[4]
    p[pl.ds(HP, NXB)] = p1[...]
    p[pl.ds(core * (HP + NXB), HP)] = off[...]
    p[pl.ds((1 - core) * (HP + NXB), HP)] = on[...]
    smooth(1, WN - 1, p, q, tw, wt, inv)
    correct(q, tw, wt, dg, lo, ca, cb, cw, cinv)
    smooth(HP - 1, HP + NXB + 1, q, p, tw, wt, inv)

    def finish_pair(j):
        sums = [None, None, None]
        held = []
        for i in (2 * j, 2 * j + 1):
            v = quad(p, i + HP)
            sides = near(v, fix)
            xu, xd = quad(p, i + HP + 1), quad(p, i + HP - 1)
            m = quad(mw, i + HP)
            up = (sides[0], xu, sides[2])
            down = (sides[1], xd, sides[3])
            for c in range(3):
                a = quad(pred, c, i)
                for zp, yp in QUAD:
                    e = a[zp][yp] - (0.5 * m[zp][yp]) * (up[c][zp][yp] - down[c][zp][yp])
                    held.append((c, i, zp, yp, e))
                    sums[c] = e if sums[c] is None else sums[c] + e
        means = [0.125 * s for s in sums]
        for c, i, zp, yp, e in held:
            put(base, (c, i), zp, yp, e - means[c])
        for c in range(3):
            plain[pl.ds((c * 8 + j) * 8, 8), :] = means[c] - gs[c, j]

    loop(0, NXB // 2, finish_pair, 4)
    for j in range(NXB // 2):
        plain[192 + 8 * j : 200 + 8 * j, :] = mc[HP // 2 + j]
    packed = jnp.dot(plain[...], parity_matrix(), precision=HIGH, preferred_element_type=F32)
    plain[...] = packed
    for half in (0, 1):
        g = plain[pl.ds(192 + 8 * (4 * half + row), 8), :]
        for chip in range(4):
            for l in range(4):
                at = (min(chip, 2) * 8 + 4 * half + l) * 8
                for to in range(4):
                    send[to, chip, half, l] = packed[at : at + 8, :]
            for to in range(4):
                send[to, chip, half, 4] = g


NC = 64
PAD = 9
ROWS = 592


def at_layer(i, off=0):
    return pl.ds(PAD * i + 1 + off, 8)


class Pack:
    def __init__(self):
        j = iota(1)
        self.low = j < 64
        self.not_first = lax.rem(j, 64) > 0
        self.not_last = lax.rem(j, 64) < 63

    def join(self, one, two):
        return jnp.where(self.low, one, pltpu.roll(two, 64, 1)), jnp.where(self.low, pltpu.roll(one, 64, 1), two)


def substep(a, b, wa, wb, pack, begin):
    held = {}

    def pair(i):
        if i not in held:
            held[i] = (a[at_layer(i), :], a[at_layer(32 + i), :])
        return held[i]

    def ends(i, keep_low):
        zero = jnp.zeros((8, 128), F32)
        out = []
        for odd in (0, 1):
            r = pltpu.roll(a[at_layer(32 * odd + i), :], 64, 1)
            out.append(jnp.where(pack.low, r, zero) if keep_low else jnp.where(pack.low, zero, r))
        return out

    for n in range(32):
        i = (begin + n) % 32
        here = pair(i)
        down = pair(i - 1) if i > 0 else ends(31, False)
        up = pair(i + 1) if i < 31 else ends(0, True)
        sides = (
            jnp.where(pack.not_first, pltpu.roll(here[1], 1, 1), 0.0),
            jnp.where(pack.not_last, pltpu.roll(here[0], 127, 1), 0.0),
        )
        for odd in (0, 1):
            at = 32 * odd + i
            total = (a[at_layer(at, 1), :] + a[at_layer(at, -1), :]) + (up[odd] + down[odd])
            total = total + (here[1 - odd] + sides[odd])
            b[at_layer(at), :] = wa[at] * here[odd] + wb[at] * total
        held.pop(i - 1, None)


def advance(times, a, b, wa, wb, pack):
    each = 2 if times % 2 == 0 else 1

    def turn(t, carry):
        for k in range(each):
            substep(a, b, wa, wb, pack, 4 * k)
            substep(b, a, wa, wb, pack, 4 * k + 2)
        return carry

    if times == each:
        turn(0, 0)
    else:
        lax.fori_loop(0, times // each, turn, 0)


def take_half(half, src, core):
    for odd in (0, 1):
        half[16 * odd : 16 * odd + 16] = src[pl.ds(32 * odd + 16 * core, 16)]


def rows_scan(info, got, swapped, acc, half, wa, wb, a, b):
    pack = Pack()
    core, row = info[0], info[4]
    a[...] = jnp.zeros_like(a)
    b[...] = jnp.zeros_like(b)

    def each(fn):
        for s in range(4):
            for l in range(4):
                for part, src in ((core, got), (1 - core, swapped)):
                    fn(s, l, 8 * s + 4 * part + l, src)

    def begin(s, l, at, src):
        even, odd = pack.join(src[l, s, 4], src[l, s + 4, 4])
        for base, m in ((0, even), (32, odd)):
            wa[base + at] = 1.0 - 0.9 * m
            wb[base + at] = 0.15 * m
        even, odd = pack.join(src[0, s, l], src[0, s + 4, l])
        a[at_layer(at), :] = even
        a[at_layer(32 + at), :] = odd

    each(begin)
    for t in range(1, 4):

        @pl.when(t <= row)
        def _():
            advance(8, a, b, wa, wb, pack)

            def include(s, l, at, src):
                even, odd = pack.join(src[t, s, l], src[t, s + 4, l])
                a[at_layer(at), :] = a[at_layer(at), :] + even
                a[at_layer(32 + at), :] = a[at_layer(32 + at), :] + odd

            each(include)

    for i in range(NC):
        acc[i] = a[at_layer(i), :]
    take_half(half, acc, core)


def load_halves(a, own, other, core, add):
    for odd in (0, 1):
        for i in range(16):
            for part, src in ((core, own), (1 - core, other)):
                at = at_layer(32 * odd + 16 * part + i)
                value = src[16 * odd + i]
                a[at, :] = a[at, :] + value if add else value


def one_scan(info, acc, own, other, wa, wb, out, half, a, b):
    pack = Pack()
    core = info[0]
    a[...] = jnp.zeros_like(a)
    b[...] = jnp.zeros_like(b)
    load_halves(a, own, other, core, False)
    advance(1, a, b, wa, wb, pack)
    for i in range(NC):
        out[i] = acc[i] + a[at_layer(i), :]
    take_half(half, out, core)


def even_scan(info, acc, own, other, wa, wb, chunk, out, a, b):
    pack = Pack()
    core = info[0]
    a[...] = jnp.zeros_like(a)
    b[...] = jnp.zeros_like(b)
    load_halves(a, own.at[2], other.at[2], core, False)
    advance(2, a, b, wa, wb, pack)
    load_halves(a, own.at[1], other.at[1], core, True)
    advance(2, a, b, wa, wb, pack)
    load_halves(a, own.at[0], other.at[0], core, True)
    advance(2, a, b, wa, wb, pack)
    for i in range(NC):
        out[i] = acc[i] + a[at_layer(i), :]
    for s in range(4):
        for l in range(4):
            at = 8 * s + 4 * core + l
            one, two = pack.join(out[at], out[32 + at])
            chunk[s, l] = one
            chunk[s + 4, l] = two


def tiles(a):
    return a.reshape(-1, 32, 8, 2, 128).transpose(0, 1, 3, 2, 4).reshape(-1, 512, 128)


def body(ny, nz, start_states, labels):
    ns = lax.axis_size("space")
    s = lax.axis_index("space")
    y = lax.axis_index("y")
    z = lax.axis_index("z")
    core = lax.rem(s, 2)
    info = jnp.stack([core, s > 0, s < ns - 1, y * nz + z > 0, y, s, s, s]).astype(jnp.int32)
    swap = [(i, i ^ 1) for i in range(ns)]
    cross = [(i, i + 1) for i in range(1, ns - 1, 2)]
    cross = cross + [(b, a) for a, b in cross]

    def exchange(outer, inner):
        off = lax.ppermute(outer, "space", cross)
        on = lax.ppermute(inner, "space", swap)
        return off, on

    start = tiles(start_states.reshape(3, 512, 128))
    label = tiles(labels.reshape(1, 16 * NXB, 256))[0]
    layer = (2, 8, 256)
    vm = lambda *d: pltpu.VMEM(d, F32)
    window = shape(WN, *layer)
    edge = shape(HP, *layer)
    both = shape(3 * HS + HP, *layer)
    s_own, m_own, outer, inner = call(
        prepare,
        [shape(3, NXB, *layer), shape(NXB, *layer), both, both],
        [info, start, label],
        [vm(3, 512, 128), pltpu.VMEM((512, 128), jnp.int32), vm(4, 256, 256), pltpu.SemaphoreType.DMA((4,))],
        ANY,
    )
    off, on = exchange(outer, inner)
    held = call(
        weights,
        [window, shape(6, WN, *layer), window, window, shape(CN, 8, 128), shape(6, CN, 8, 128), shape(CN, 8, 128)],
        [info, m_own, off, on],
    )
    coarse = [vm(CN, 8, 128)] * 3
    pred, tw, p1, outer, inner, gs = call(
        first_cycle,
        [shape(3, NXB, *layer), window, shape(NXB, *layer), edge, edge, shape(3, 8, 8, 128)],
        [info, s_own, off, on] + list(held),
        [vm(3, NXB + 2 * HS, *layer), vm(3, WN, *layer), vm(WN, *layer)] + coarse + [vm(3, 12, 8, 128)] * 2,
    )
    off, on = exchange(outer, inner)
    base, send = call(
        second_cycle,
        [shape(3, NXB, *layer), shape(4, 4, 2, 5, 8, 128)],
        [info, pred, tw, p1, off, on, gs] + list(held),
        [vm(WN, *layer)] * 2 + coarse + [vm(256, 128)],
    )
    got = lax.all_to_all(send.reshape(ny * ns, 5, 8, 128), ("y", "space"), 0, 0)
    got = got.reshape(ny, ns, 5, 8, 128)
    swapped = lax.ppermute(got, "space", swap)
    acc, half, wa, wb = call(
        rows_scan,
        [shape(NC, 8, 128), shape(NC // 2, 8, 128), shape(NC, 8, 128), shape(NC, 8, 128)],
        [info, got, swapped],
        [vm(ROWS, 128)] * 2,
    )
    nt = ny * nz

    def shifted(value, k):
        return lax.ppermute(value, ("y", "z"), [(i, i + k) for i in range(nt - k)])

    own = shifted(half, 1)
    other = lax.ppermute(own, "space", swap)
    state = [vm(ROWS, 128)] * 2
    acc, half = call(
        one_scan, [shape(NC, 8, 128), shape(NC // 2, 8, 128)], [info, acc, own, other, wa, wb], state
    )
    own = jnp.stack([shifted(half, k) for k in (2, 4, 6)])
    other = lax.ppermute(own, "space", swap)
    (chunks,) = call(
        even_scan, [shape(8, 4, 8, 128)], [info, acc, own, other, wa, wb], [vm(NC, 8, 128)] + state
    )
    (nat,) = call(interleave, [shape(3, 512, 128)], [base])
    back = lax.all_to_all(chunks, "space", 0, 0)
    w = back[:6].reshape(3, 8, 8, 128)
    (out,) = call(finish, [shape(3, 512, 128)], [nat, w])
    out = out.reshape(3, 32, 2, 8, 128).transpose(0, 1, 3, 2, 4)
    return out.reshape(1, 3, 16, NXB, 256)


def solution(mesh):
    nz = 8
    ny = mesh.shape["tm"] // nz
    split = Mesh(mesh.devices.reshape(ny, nz, mesh.shape["space"]), ("y", "z", "space"))
    in_specs = (P(("y", "z"), None, None, "space", None), P(None, "space", None))
    out_specs = P(("y", "z"), None, None, "space", None)

    def run(start_states, labels):
        return body(ny, nz, start_states, labels)

    return jax.shard_map(run, mesh=split, in_specs=in_specs, out_specs=out_specs, check_vma=False)
```

```python
import jax
import jax.numpy as jnp
from jax import lax
from jax.experimental import pallas as pl
from jax.experimental.pallas import tpu as pltpu
from jax.sharding import Mesh, PartitionSpec as P

F32 = jnp.float32
VM = pl.BlockSpec(memory_space=pltpu.VMEM)
SM = pl.BlockSpec(memory_space=pltpu.SMEM)
ANY = pl.BlockSpec(memory_space=pltpu.HBM)

NXB = 16
HS = 11
HP = 10
WN = NXB + 2 * HP
CN = WN // 2


def shape(*dims):
    return jax.ShapeDtypeStruct(dims, F32)


def call(kernel, outs, ins, scratch=(), where=VM, to=VM, aliases={}):
    specs = [SM if a.dtype == jnp.int32 and a.ndim == 1 else where for a in ins]
    moved = sum(a.size * 4 for a in ins) + sum(4 * _size(o) for o in outs)
    return pl.pallas_call(
        kernel,
        out_shape=outs,
        in_specs=specs,
        out_specs=[to] * len(outs),
        scratch_shapes=list(scratch),
        input_output_aliases=aliases,
        compiler_params=pltpu.CompilerParams(vmem_limit_bytes=28 * 1024 * 1024),
        cost_estimate=pl.CostEstimate(flops=1000000, bytes_accessed=moved, transcendentals=0),
    )(*ins)


def _size(o):
    n = 1
    for d in o.shape:
        n *= d
    return n


def loop(lo, hi, fn, unroll=0):
    unroll = unroll or hi - lo
    if unroll == hi - lo:
        for i in range(lo, hi):
            fn(i)
        return
    assert (hi - lo) % unroll == 0

    def step(t, carry):
        for u in range(unroll):
            fn(lo + t * unroll + u)
        return carry

    lax.fori_loop(0, (hi - lo) // unroll, step, 0)


def iota(dim):
    return lax.broadcasted_iota(jnp.int32, (8, 128), dim)


def quad(ref, *at):
    return [[ref[(*at, zp, slice(None), slice(128 * yp, 128 * yp + 128))] for yp in (0, 1)] for zp in (0, 1)]


def put(ref, at, zp, yp, value):
    ref[(*at, zp, slice(None), slice(128 * yp, 128 * yp + 128))] = value


def z_up(v, fix=None):
    f = fix or (lambda r: r)
    return [v[1], [f(pltpu.roll(v[0][q], 7, 0)) for q in (0, 1)]]


def z_down(v, fix=None):
    f = fix or (lambda r: r)
    return [[f(pltpu.roll(v[1][q], 1, 0)) for q in (0, 1)], v[0]]


def y_up(v, fix=None):
    f = fix or (lambda r: r)
    return [[v[q][1], f(pltpu.roll(v[q][0], 127, 1))] for q in (0, 1)]


def y_down(v, fix=None):
    f = fix or (lambda r: r)
    return [[f(pltpu.roll(v[q][1], 1, 1)), v[q][0]] for q in (0, 1)]


class Fix:
    def __init__(self):
        k, j = iota(0), iota(1)
        self.zu = lambda r: jnp.where(k < 7, r, 0.0)
        self.zd = lambda r: jnp.where(k > 0, r, 0.0)
        self.yu = lambda r: jnp.where(j < 127, r, 0.0)
        self.yd = lambda r: jnp.where(j > 0, r, 0.0)


def coarse_near(v, fix):
    return (
        fix.zu(pltpu.roll(v, 7, 0)),
        fix.zd(pltpu.roll(v, 1, 0)),
        fix.yu(pltpu.roll(v, 127, 1)),
        fix.yd(pltpu.roll(v, 1, 1)),
    )


def near(v, fix):
    return (z_up(v, fix.zu), z_down(v, fix.zd), y_up(v, fix.yu), y_down(v, fix.yd))


def raw_near(v):
    return (z_up(v), z_down(v), y_up(v), y_down(v))


QUAD = [(zp, yp) for zp in (0, 1) for yp in (0, 1)]


def eight(ref, i):
    total = None
    for layer in (i, i + 1):
        v = quad(ref, layer)
        for zp, yp in QUAD:
            total = v[zp][yp] if total is None else total + v[zp][yp]
    return total


def exact_dot(x, chooser):
    one = x.astype(jnp.bfloat16)
    rest = x - one.astype(F32)
    two = rest.astype(jnp.bfloat16)
    three = (rest - two.astype(F32)).astype(jnp.bfloat16)
    dot = lambda part: jnp.dot(part, chooser, preferred_element_type=F32)
    return (dot(three) + dot(two)) + dot(one)


def split_matrix():
    r = lax.broadcasted_iota(jnp.int32, (256, 256), 0)
    c = lax.broadcasted_iota(jnp.int32, (256, 256), 1)
    return jnp.where(r == jnp.where(c < 128, 2 * c, 2 * c - 255), 1.0, 0.0).astype(jnp.bfloat16)


def join_matrix():
    r = lax.broadcasted_iota(jnp.int32, (256, 256), 0)
    c = lax.broadcasted_iota(jnp.int32, (256, 256), 1)
    return jnp.where(c == jnp.where(r < 128, 2 * r, 2 * r - 255), 1.0, 0.0).astype(jnp.bfloat16)


def parity_matrix():
    r = lax.broadcasted_iota(jnp.int32, (128, 128), 0)
    c = lax.broadcasted_iota(jnp.int32, (128, 128), 1)
    return jnp.where(r == jnp.where(c < 64, 2 * c, 2 * c - 127), 1.0, 0.0).astype(jnp.bfloat16)


def rows_of(x, zp, q):
    return pl.ds((4 * zp + 2 * (x // 8) + q) * 8 + x % 8, 8, stride=64)


def prepare(info, start, labels, s_out, m_out, outer, inner, s_in, l_in, rows, sems):
    core = info[0]
    copies = [pltpu.make_async_copy(labels, l_in, sems.at[3])]
    copies += [pltpu.make_async_copy(start.at[c], s_in.at[c], sems.at[c]) for c in range(3)]
    for copy in copies:
        copy.start()
    split = split_matrix()
    copies[0].wait()
    for x in range(NXB):
        for zp in (0, 1):
            for q in (0, 1):
                mobility = 1.0 / (1.0 + 3.0 * l_in[rows_of(x, zp, q), :].astype(F32))
                rows[3, pl.ds((x * 2 + zp) * 8, 8), 128 * q : 128 * q + 128] = mobility
    done = jnp.dot(rows[3].astype(jnp.bfloat16), split, preferred_element_type=F32)
    m_out[...] = done.reshape(NXB, 2, 8, 256)
    outer[pl.ds(3 * HS, HP)] = m_out[pl.ds((NXB - HP) * core, HP)]
    inner[pl.ds(3 * HS, HP)] = m_out[pl.ds((NXB - HP) * (1 - core), HP)]
    for c in range(3):
        copies[1 + c].wait()
        for x in range(NXB):
            for zp in (0, 1):
                for q in (0, 1):
                    rows[c, pl.ds((x * 2 + zp) * 8, 8), 128 * q : 128 * q + 128] = s_in[c, rows_of(x, zp, q), :]
        done = exact_dot(rows[c], split)
        s_out[c] = done.reshape(NXB, 2, 8, 256)
        outer[pl.ds(c * HS, HS)] = s_out[c, pl.ds((NXB - HS) * core, HS)]
        inner[pl.ds(c * HS, HS)] = s_out[c, pl.ds((NXB - HS) * (1 - core), HS)]


def interleave(base, nat):
    join = join_matrix()
    for c in range(3):
        done = exact_dot(base[c].reshape(256, 256), join)
        for x in range(NXB):
            for zp in (0, 1):
                at = (x * 2 + zp) * 8
                for q in (0, 1):
                    cols = slice(128 * q, 128 * q + 128)
                    nat[c, rows_of(x, zp, q), :] = done[at : at + 8, cols]


def finish(nat, w, out, made, sems):
    r = lax.broadcasted_iota(jnp.int32, (128, 256), 0)
    c = lax.broadcasted_iota(jnp.int32, (128, 256), 1)
    spread = jnp.where(lax.div(c, 2) == jnp.where(r < 64, 2 * r, 2 * r - 127), 1.0, 0.0).astype(jnp.bfloat16)
    done = exact_dot(w[...].reshape(192, 128), spread)
    copies = []
    for comp in range(3):
        for xc in range(NXB // 2):
            at = (comp * 8 + xc) * 8
            for q in (0, 1):
                cols = slice(128 * q, 128 * q + 128)
                value = done[at : at + 8, cols]
                for xp in (0, 1):
                    for zp in (0, 1):
                        sl = rows_of(2 * xc + xp, zp, q)
                        made[comp, sl, :] = nat[comp, sl, :] + value
        copies.append(pltpu.make_async_copy(made.at[comp], out.at[comp], sems.at[comp]))
        copies[-1].start()
    for copy in copies:
        copy.wait()


def valid_of(info):
    left, right = info[1].astype(F32), info[2].astype(F32)
    return lambda i, halo: jnp.where(i < halo, left, jnp.where(i >= halo + NXB, right, jnp.float32(1.0)))


def weigh(valid, mw, wt, dg, inv, mc, cw, cinv, fix, inside):
    def layer(i):
        m = quad(mw, i)
        sides = near(m, fix) + (quad(mw, i + 1), quad(mw, i - 1))
        ok = valid(i, HP)
        for zp, yp in QUAD:
            faces = [0.5 * (m[zp][yp] + s[zp][yp]) for s in sides]
            total = faces[0] + faces[1] + faces[2] + faces[3] + faces[4] + faces[5]
            if zp == 1:
                faces[0] = fix.zu(faces[0])
            else:
                faces[1] = fix.zd(faces[1])
            if yp == 1:
                faces[2] = fix.yu(faces[2])
            else:
                faces[3] = fix.yd(faces[3])
            for f in range(6):
                put(wt, (f, i), zp, yp, faces[f])
            put(dg, (i,), zp, yp, total)
            put(inv, (i,), zp, yp, (0.8 * ok) / (total + (1.0 - ok)))

    if inside:
        loop(HP + 1, HP + NXB - 1, layer, 7)
    else:
        loop(1, HP + 1, layer)
        loop(HP + NXB - 1, WN - 1, layer)

    def coarse(j):
        mc[j] = 0.125 * eight(mw, 2 * j)

    mine = range(HP // 2, HP // 2 + NXB // 2)
    for j in range(CN):
        if (j in mine) == inside:
            coarse(j)

    def coarse_layer(j):
        m = mc[j]
        sides = coarse_near(m, fix) + (mc[j + 1], mc[j - 1])
        ok = valid(2 * j, HP)
        faces = [0.125 * (m + s) for s in sides]
        total = faces[0] + faces[1] + faces[2] + faces[3] + faces[4] + faces[5]
        faces[0] = fix.zu(faces[0])
        faces[1] = fix.zd(faces[1])
        faces[2] = fix.yu(faces[2])
        faces[3] = fix.yd(faces[3])
        for f in range(6):
            cw[f, j] = faces[f]
        cinv[j] = (0.8 * ok) / (total + (1.0 - ok))

    mine = range(HP // 2 + 1, HP // 2 + NXB // 2 - 1)
    for j in range(1, CN - 1):
        if (j in mine) == inside:
            coarse_layer(j)


def predicting(valid, mw, sw, at, pr, fix):
    def predict(i):
        ok = valid(i, HP)
        m = quad(mw, i)
        for c in range(3):
            v = quad(sw, c, i + 1 - at)
            sides = near(v, fix) + (quad(sw, c, i + 2 - at), quad(sw, c, i - at))
            for zp, yp in QUAD:
                n = [s[zp][yp] for s in sides]
                total = ((n[0] + n[1]) + (n[2] + n[3])) + (n[4] + n[5])
                value = 0.4 * v[zp][yp] + 0.1 * total
                if c == 0:
                    value = value + (0.4 * m[zp][yp] - 0.2)
                put(pr, (c, i), zp, yp, ok * value)

    return predict


def gathered(p, i, wt):
    v = quad(p, i)
    sides = raw_near(v) + (quad(p, i + 1), quad(p, i - 1))
    ws = [quad(wt, f, i) for f in range(6)]
    total = [[None, None], [None, None]]
    for zp, yp in QUAD:
        terms = [ws[f][zp][yp] * sides[f][zp][yp] for f in range(6)]
        total[zp][yp] = ((terms[0] + terms[1]) + (terms[2] + terms[3])) + (terms[4] + terms[5])
    return v, total


def smooth(lo, hi, p, q, tw, wt, inv):
    def layer(i):
        v, total = gathered(p, i, wt)
        t, n = quad(tw, i), quad(inv, i)
        for zp, yp in QUAD:
            put(q, (i,), zp, yp, 0.2 * v[zp][yp] + n[zp][yp] * (t[zp][yp] + total[zp][yp]))

    loop(lo, hi, layer, (hi - lo) // 2)


def correct(p, tw, wt, dg, lo, ca, cb, cw, cinv):
    def coarse(j):
        out = None
        for i in (2 * j, 2 * j + 1):
            v, total = gathered(p, i, wt)
            t, d = quad(tw, i), quad(dg, i)
            for zp, yp in QUAD:
                r = (t[zp][yp] + total[zp][yp]) - d[zp][yp] * v[zp][yp]
                out = r if out is None else out + r
        out = 0.125 * out
        lo[j] = out
        ca[j] = cinv[j] * out

    loop(1, CN - 1, coarse, 8)

    def sweep(first, last, a, b):
        def layer(j):
            v = a[j]
            sides = (
                pltpu.roll(v, 7, 0),
                pltpu.roll(v, 1, 0),
                pltpu.roll(v, 127, 1),
                pltpu.roll(v, 1, 1),
                a[j + 1],
                a[j - 1],
            )
            terms = [cw[f, j] * sides[f] for f in range(6)]
            total = ((terms[0] + terms[1]) + (terms[2] + terms[3])) + (terms[4] + terms[5])
            b[j] = 0.2 * v + cinv[j] * (lo[j] + total)

        loop(first, last, layer)

    sweep(2, CN - 2, ca, cb)
    sweep(3, CN - 3, cb, ca)
    sweep(4, CN - 4, ca, cb)

    def add(j):
        g = cb[j]
        for i in (2 * j, 2 * j + 1):
            v = quad(p, i)
            for zp, yp in QUAD:
                put(p, (i,), zp, yp, v[zp][yp] + g)

    loop(4, CN - 4, add)


def inside(info, s_own, m_own, mw, wt, dg, inv, mc, cw, cinv, pr):
    fix = Fix()
    valid = valid_of(info)
    mw[pl.ds(HP, NXB)] = m_own[...]
    weigh(valid, mw, wt, dg, inv, mc, cw, cinv, fix, True)
    loop(HP + 1, HP + NXB - 1, predicting(valid, mw, s_own, HS, pr, fix), 7)


def first_cycle(info, s_own, off, on, *refs):
    mw, wt, dg, inv, mc, cw, cinv, pr, pred, tw, p1, outer, inner, gs, sw, p, lo, ca, cb, rs, rt = refs[8:]
    fix = Fix()
    core = info[0]
    valid = valid_of(info)
    off_s, on_s = core * (HS + NXB), (1 - core) * (HS + NXB)
    for c in range(3):
        sw[c, pl.ds(HS, NXB)] = s_own[c]
        sw[c, pl.ds(off_s, HS)] = off[pl.ds(c * HS, HS)]
        sw[c, pl.ds(on_s, HS)] = on[pl.ds(c * HS, HS)]
    mw[pl.ds(core * (HP + NXB), HP)] = off[pl.ds(3 * HS, HP)]
    mw[pl.ds((1 - core) * (HP + NXB), HP)] = on[pl.ds(3 * HS, HP)]
    weigh(valid, mw, wt, dg, inv, mc, cw, cinv, fix, False)
    predict = predicting(valid, mw, sw, 0, pr, fix)
    loop(0, HP + 1, predict)
    loop(HP + NXB - 1, WN, predict)

    def aim(i):
        a, b = quad(pr, 0, i), quad(pr, 2, i)
        zu, zd = z_up(a, fix.zu), z_down(a, fix.zd)
        yu, yd = y_up(b, fix.yu), y_down(b, fix.yd)
        xu, xd = quad(pr, 1, i + 1), quad(pr, 1, i - 1)
        n = quad(inv, i)
        for zp, yp in QUAD:
            t = (zu[zp][yp] - zd[zp][yp]) + (xu[zp][yp] - xd[zp][yp])
            t = -0.5 * (t + (yu[zp][yp] - yd[zp][yp]))
            put(tw, (i,), zp, yp, t)
            put(p, (i,), zp, yp, n[zp][yp] * t)

    loop(1, WN - 1, aim, 17)
    for c in range(3):
        pred[c] = pr[c, pl.ds(HP, NXB)]

    correct(p, tw, wt, dg, lo, ca, cb, cw, cinv)

    def last(x):
        i = x + HP
        v, total = gathered(p, i, wt)
        t, n = quad(tw, i), quad(inv, i)
        for zp, yp in QUAD:
            put(p1, (x,), zp, yp, 0.2 * v[zp][yp] + n[zp][yp] * (t[zp][yp] + total[zp][yp]))

    loop(0, NXB, last, 8)
    outer[...] = p1[pl.ds((NXB - HP) * core, HP)]
    inner[...] = p1[pl.ds((NXB - HP) * (1 - core), HP)]

    later = info[3].astype(F32)

    def shrink(q):
        for c in range(3):
            rs[c, q] = 0.125 * eight(sw.at[c], 2 * q + 7)

    loop(0, 12, shrink)

    def coarse_step(a, b, scale):
        def layer(q):
            m = mc[q + 3]
            for c in range(3):
                v = a[c, q]
                n = coarse_near(v, fix) + (a[c, q + 1], a[c, q - 1])
                total = ((n[0] + n[1]) + (n[2] + n[3])) + (n[4] + n[5])
                b(c, q, scale * ((1.0 - 0.9 * m) * v + (0.15 * m) * total))

        return layer

    def to_rt(c, q, value):
        rt[c, q] = value

    def to_gs(c, q, value):
        gs[c, q - 2] = value

    loop(1, 11, coarse_step(rs, to_rt, 1.0))
    loop(2, 10, coarse_step(rt, to_gs, later))


def second_cycle(info, pred, tw, p1, off, on, gs, mw, wt, dg, inv, mc, cw, cinv, base, send, p, q, lo, ca, cb, plain):
    fix = Fix()
    core, row = info[0], info[4]
    p[pl.ds(HP, NXB)] = p1[...]
    p[pl.ds(core * (HP + NXB), HP)] = off[...]
    p[pl.ds((1 - core) * (HP + NXB), HP)] = on[...]
    smooth(1, WN - 1, p, q, tw, wt, inv)
    correct(q, tw, wt, dg, lo, ca, cb, cw, cinv)
    smooth(HP - 1, HP + NXB + 1, q, p, tw, wt, inv)

    def finish_pair(j):
        sums = [None, None, None]
        held = []
        for i in (2 * j, 2 * j + 1):
            v = quad(p, i + HP)
            sides = near(v, fix)
            xu, xd = quad(p, i + HP + 1), quad(p, i + HP - 1)
            m = quad(mw, i + HP)
            up = (sides[0], xu, sides[2])
            down = (sides[1], xd, sides[3])
            for c in range(3):
                a = quad(pred, c, i)
                for zp, yp in QUAD:
                    e = a[zp][yp] - (0.5 * m[zp][yp]) * (up[c][zp][yp] - down[c][zp][yp])
                    held.append((c, i, zp, yp, e))
                    sums[c] = e if sums[c] is None else sums[c] + e
        means = [0.125 * s for s in sums]
        for c, i, zp, yp, e in held:
            put(base, (c, i), zp, yp, e - means[c])
        for c in range(3):
            plain[pl.ds((c * 8 + j) * 8, 8), :] = means[c] - gs[c, j]

    loop(0, NXB // 2, finish_pair, 4)
    for j in range(NXB // 2):
        plain[192 + 8 * j : 200 + 8 * j, :] = mc[HP // 2 + j]
    packed = exact_dot(plain[...], parity_matrix())
    plain[...] = packed
    for half in (0, 1):
        g = plain[pl.ds(192 + 8 * (4 * half + row), 8), :]
        for chip in range(4):
            for l in range(4):
                at = (min(chip, 2) * 8 + 4 * half + l) * 8
                for to in range(4):
                    send[to, chip, half, l] = packed[at : at + 8, :]
            for to in range(4):
                send[to, chip, half, 4] = g


NC = 64
PAD = 9
ROWS = 592


def at_layer(i, off=0):
    return pl.ds(PAD * i + 1 + off, 8)


class Pack:
    def __init__(self):
        j = iota(1)
        self.low = j < 64
        self.not_first = lax.rem(j, 64) > 0
        self.not_last = lax.rem(j, 64) < 63

    def join(self, one, two):
        return jnp.where(self.low, one, pltpu.roll(two, 64, 1)), jnp.where(self.low, pltpu.roll(one, 64, 1), two)


def substep(a, b, wa, wb, pack, begin):
    held = {}

    def pair(i):
        if i not in held:
            held[i] = (a[at_layer(i), :], a[at_layer(32 + i), :])
        return held[i]

    def ends(i, keep_low):
        zero = jnp.zeros((8, 128), F32)
        out = []
        for odd in (0, 1):
            r = pltpu.roll(a[at_layer(32 * odd + i), :], 64, 1)
            out.append(jnp.where(pack.low, r, zero) if keep_low else jnp.where(pack.low, zero, r))
        return out

    for n in range(32):
        i = (begin + n) % 32
        here = pair(i)
        down = pair(i - 1) if i > 0 else ends(31, False)
        up = pair(i + 1) if i < 31 else ends(0, True)
        sides = (
            jnp.where(pack.not_first, pltpu.roll(here[1], 1, 1), 0.0),
            jnp.where(pack.not_last, pltpu.roll(here[0], 127, 1), 0.0),
        )
        for odd in (0, 1):
            at = 32 * odd + i
            total = (a[at_layer(at, 1), :] + a[at_layer(at, -1), :]) + (up[odd] + down[odd])
            total = total + (here[1 - odd] + sides[odd])
            b[at_layer(at), :] = wa[at] * here[odd] + wb[at] * total
        held.pop(i - 1, None)


def advance(times, a, b, wa, wb, pack):
    each = 4 if times % 4 == 0 else times

    def turn(t, carry):
        for k in range(each):
            substep(a, b, wa, wb, pack, 4 * k)
            substep(b, a, wa, wb, pack, 4 * k + 2)
        return carry

    if times == each:
        turn(0, 0)
    else:
        lax.fori_loop(0, times // each, turn, 0)


def take_half(half, src, core):
    for odd in (0, 1):
        half[16 * odd : 16 * odd + 16] = src[pl.ds(32 * odd + 16 * core, 16)]


def rows_scan(info, got, swapped, acc, to, wa, wb, a, b, half, before):
    pack = Pack()
    core, row, quarter = info[0], info[4], info[5]
    before[...] = jnp.zeros_like(before)
    a[...] = jnp.zeros_like(a)
    b[...] = jnp.zeros_like(b)

    def each(fn):
        for s in range(4):
            for l in range(4):
                for part, src in ((core, got), (1 - core, swapped)):
                    fn(s, l, 8 * s + 4 * part + l, src)

    def begin(s, l, at, src):
        even, odd = pack.join(src[l, s, 4], src[l, s + 4, 4])
        for base, m in ((0, even), (32, odd)):
            wa[base + at] = 1.0 - 0.9 * m
            wb[base + at] = 0.15 * m
        even, odd = pack.join(src[0, s, l], src[0, s + 4, l])
        a[at_layer(at), :] = even
        a[at_layer(32 + at), :] = odd

    each(begin)
    for t in range(1, 4):

        @pl.when(t <= row)
        def _():
            for odd in (0, 1):
                for i in range(16):
                    before[16 * odd + i] = a[at_layer(32 * odd + 16 * core + i), :]
            advance(8, a, b, wa, wb, pack)

            def include(s, l, at, src):
                even, odd = pack.join(src[t, s, l], src[t, s + 4, l])
                a[at_layer(at), :] = a[at_layer(at), :] + even
                a[at_layer(32 + at), :] = a[at_layer(32 + at), :] + odd

            each(include)

    for i in range(NC):
        acc[i] = a[at_layer(i), :]
    take_half(half, acc, core)
    for d in range(4):

        @pl.when(d >= quarter)
        def _():
            to[d] = half[...]

        @pl.when(d < quarter)
        def _():
            to[d] = before[...]


def load_halves(a, own, other, core, add):
    for odd in (0, 1):
        for i in range(16):
            for part, src in ((core, own), (1 - core, other)):
                at = at_layer(32 * odd + 16 * part + i)
                value = src[16 * odd + i]
                a[at, :] = a[at, :] + value if add else value


def even_scan(info, acc, own, other, wa, wb, out, half, a, b):
    pack = Pack()
    core, quarter = info[0], info[5]
    a[...] = jnp.zeros_like(a)
    b[...] = jnp.zeros_like(b)
    for back in (3, 2, 1):
        src = lax.rem(quarter + 4 - back, 4)
        load_halves(a, own.at[src], other.at[src], core, back < 3)
        advance(2, a, b, wa, wb, pack)
    for i in range(NC):
        out[i] = acc[i] + a[at_layer(i), :]
    take_half(half, out, core)


def one_scan(info, acc, own, other, wa, wb, chunk, out, a, b):
    pack = Pack()
    core = info[0]
    a[...] = jnp.zeros_like(a)
    b[...] = jnp.zeros_like(b)
    load_halves(a, own, other, core, False)
    advance(1, a, b, wa, wb, pack)
    for i in range(NC):
        out[i] = acc[i] + a[at_layer(i), :]
    for s in range(4):
        for l in range(4):
            at = 8 * s + 4 * core + l
            one, two = pack.join(out[at], out[32 + at])
            chunk[s, l] = one
            chunk[s + 4, l] = two


def tiles(a):
    return a.reshape(-1, 32, 8, 2, 128).transpose(0, 1, 3, 2, 4).reshape(-1, 512, 128)


def body(ny, nz, start_states, labels):
    ns = lax.axis_size("space")
    s = lax.axis_index("space")
    y = lax.axis_index("y")
    quarter = lax.axis_index("zq")
    z = 2 * quarter + lax.axis_index("zp")
    core = lax.rem(s, 2)
    info = jnp.stack([core, s > 0, s < ns - 1, y * nz + z > 0, y, quarter, s, s]).astype(jnp.int32)
    swap = [(i, i ^ 1) for i in range(ns)]
    cross = [(i, i + 1) for i in range(1, ns - 1, 2)]
    cross = cross + [(b, a) for a, b in cross]

    def exchange(outer, inner):
        off = lax.ppermute(outer, "space", cross)
        on = lax.ppermute(inner, "space", swap)
        return off, on

    start = tiles(start_states.reshape(3, 512, 128))
    label = tiles(labels.reshape(1, 16 * NXB, 256))[0]
    layer = (2, 8, 256)
    vm = lambda *d: pltpu.VMEM(d, F32)
    window = shape(WN, *layer)
    edge = shape(HP, *layer)
    both = shape(3 * HS + HP, *layer)
    s_own, m_own, outer, inner = call(
        prepare,
        [shape(3, NXB, *layer), shape(NXB, *layer), both, both],
        [info, pltpu.with_memory_space_constraint(start, pltpu.HBM), pltpu.with_memory_space_constraint(label, pltpu.HBM)],
        [vm(3, 512, 128), pltpu.VMEM((512, 128), jnp.int32), vm(4, 256, 256), pltpu.SemaphoreType.DMA((4,))],
        ANY,
    )
    off, on = exchange(outer, inner)
    kept = [window, shape(6, WN, *layer), window, window, shape(CN, 8, 128), shape(6, CN, 8, 128), shape(CN, 8, 128)]
    kept.append(shape(3, WN, *layer))
    held = call(inside, kept, [info, s_own, m_own])
    coarse = [vm(CN, 8, 128)] * 3
    done = call(
        first_cycle,
        kept + [shape(3, NXB, *layer), window, shape(NXB, *layer), edge, edge, shape(3, 8, 8, 128)],
        [info, s_own, off, on] + list(held),
        [vm(3, NXB + 2 * HS, *layer), vm(WN, *layer)] + coarse + [vm(3, 12, 8, 128)] * 2,
        aliases={4 + i: i for i in range(8)},
    )
    held, (pred, tw, p1, outer, inner, gs) = done[:7], done[8:]
    off, on = exchange(outer, inner)
    base, send = call(
        second_cycle,
        [shape(3, NXB, *layer), shape(4, 4, 2, 5, 8, 128)],
        [info, pred, tw, p1, off, on, gs] + list(held),
        [vm(WN, *layer)] * 2 + coarse + [vm(256, 128)],
    )
    got = lax.all_to_all(send.reshape(ny * ns, 5, 8, 128), ("y", "space"), 0, 0)
    got = got.reshape(ny, ns, 5, 8, 128)
    swapped = lax.ppermute(got, "space", swap)
    state = [vm(ROWS, 128)] * 2
    acc, to, wa, wb = call(
        rows_scan,
        [shape(NC, 8, 128), shape(4, NC // 2, 8, 128), shape(NC, 8, 128), shape(NC, 8, 128)],
        [info, got, swapped],
        state + [vm(NC // 2, 8, 128)] * 2,
    )
    own = lax.all_to_all(to, "zq", 0, 0)
    other = lax.ppermute(own, "space", swap)
    acc, half = call(
        even_scan, [shape(NC, 8, 128), shape(NC // 2, 8, 128)], [info, acc, own, other, wa, wb], state
    )
    nt = ny * nz
    own = lax.ppermute(half, ("y", "zq", "zp"), [(i, i + 1) for i in range(nt - 1)])
    other = lax.ppermute(own, "space", swap)
    (chunks,) = call(
        one_scan, [shape(8, 4, 8, 128)], [info, acc, own, other, wa, wb], [vm(NC, 8, 128)] + state
    )
    (nat,) = call(interleave, [shape(3, 512, 128)], [base])
    back = lax.all_to_all(chunks, "space", 0, 0)
    w = back[:6].reshape(3, 8, 8, 128)
    (out,) = call(finish, [shape(3, 512, 128)], [nat, w], [vm(3, 512, 128), pltpu.SemaphoreType.DMA((3,))], VM, ANY)
    out = out.reshape(3, 32, 2, 8, 128).transpose(0, 1, 3, 2, 4)
    return out.reshape(1, 3, 16, NXB, 256)


def solution(mesh):
    nz = 8
    ny = mesh.shape["tm"] // nz
    split = Mesh(mesh.devices.reshape(ny, nz // 2, 2, mesh.shape["space"]), ("y", "zq", "zp", "space"))
    in_specs = (P(("y", "zq", "zp"), None, None, "space", None), P(None, "space", None))
    out_specs = P(("y", "zq", "zp"), None, None, "space", None)

    def run(start_states, labels):
        return body(ny, nz, start_states, labels)

    return jax.shard_map(run, mesh=split, in_specs=in_specs, out_specs=out_specs, check_vma=False)
```

```python
import jax
import jax.numpy as jnp
from jax import lax
from jax.experimental import pallas as pl
from jax.experimental.pallas import tpu as pltpu
from jax.sharding import Mesh, PartitionSpec as P

F32 = jnp.float32
VM = pl.BlockSpec(memory_space=pltpu.VMEM)
SM = pl.BlockSpec(memory_space=pltpu.SMEM)
ANY = pl.BlockSpec(memory_space=pltpu.HBM)

NXB = 16
HS = 11
HP = 10
WN = NXB + 2 * HP
CN = WN // 2


def shape(*dims):
    return jax.ShapeDtypeStruct(dims, F32)


def call(kernel, outs, ins, scratch=(), where=VM, to=VM, aliases={}):
    specs = [SM if a.dtype == jnp.int32 and a.ndim == 1 else where for a in ins]
    moved = sum(a.size * 4 for a in ins) + sum(4 * _size(o) for o in outs)
    return pl.pallas_call(
        kernel,
        out_shape=outs,
        in_specs=specs,
        out_specs=[to] * len(outs),
        scratch_shapes=list(scratch),
        input_output_aliases=aliases,
        compiler_params=pltpu.CompilerParams(vmem_limit_bytes=28 * 1024 * 1024),
        cost_estimate=pl.CostEstimate(flops=1000000, bytes_accessed=moved, transcendentals=0),
    )(*ins)


def _size(o):
    n = 1
    for d in o.shape:
        n *= d
    return n


def loop(lo, hi, fn, unroll=0):
    unroll = unroll or hi - lo
    if unroll == hi - lo:
        for i in range(lo, hi):
            fn(i)
        return
    assert (hi - lo) % unroll == 0

    def step(t, carry):
        for u in range(unroll):
            fn(lo + t * unroll + u)
        return carry

    lax.fori_loop(0, (hi - lo) // unroll, step, 0)


def iota(dim):
    return lax.broadcasted_iota(jnp.int32, (8, 128), dim)


def quad(ref, *at):
    return [[ref[(*at, zp, slice(None), slice(128 * yp, 128 * yp + 128))] for yp in (0, 1)] for zp in (0, 1)]


def put(ref, at, zp, yp, value):
    ref[(*at, zp, slice(None), slice(128 * yp, 128 * yp + 128))] = value


def z_up(v, fix=None):
    f = fix or (lambda r: r)
    return [v[1], [f(pltpu.roll(v[0][q], 7, 0)) for q in (0, 1)]]


def z_down(v, fix=None):
    f = fix or (lambda r: r)
    return [[f(pltpu.roll(v[1][q], 1, 0)) for q in (0, 1)], v[0]]


def y_up(v, fix=None):
    f = fix or (lambda r: r)
    return [[v[q][1], f(pltpu.roll(v[q][0], 127, 1))] for q in (0, 1)]


def y_down(v, fix=None):
    f = fix or (lambda r: r)
    return [[f(pltpu.roll(v[q][1], 1, 1)), v[q][0]] for q in (0, 1)]


class Fix:
    def __init__(self):
        k, j = iota(0), iota(1)
        self.zu = lambda r: jnp.where(k < 7, r, 0.0)
        self.zd = lambda r: jnp.where(k > 0, r, 0.0)
        self.yu = lambda r: jnp.where(j < 127, r, 0.0)
        self.yd = lambda r: jnp.where(j > 0, r, 0.0)


def coarse_near(v, fix):
    return (
        fix.zu(pltpu.roll(v, 7, 0)),
        fix.zd(pltpu.roll(v, 1, 0)),
        fix.yu(pltpu.roll(v, 127, 1)),
        fix.yd(pltpu.roll(v, 1, 1)),
    )


def near(v, fix):
    return (z_up(v, fix.zu), z_down(v, fix.zd), y_up(v, fix.yu), y_down(v, fix.yd))


def raw_near(v):
    return (z_up(v), z_down(v), y_up(v), y_down(v))


QUAD = [(zp, yp) for zp in (0, 1) for yp in (0, 1)]


def eight(ref, i):
    total = None
    for layer in (i, i + 1):
        v = quad(ref, layer)
        for zp, yp in QUAD:
            total = v[zp][yp] if total is None else total + v[zp][yp]
    return total


def exact_dot(x, chooser):
    one = x.astype(jnp.bfloat16)
    rest = x - one.astype(F32)
    two = rest.astype(jnp.bfloat16)
    three = (rest - two.astype(F32)).astype(jnp.bfloat16)
    dot = lambda part: jnp.dot(part, chooser, preferred_element_type=F32)
    return (dot(three) + dot(two)) + dot(one)


def split_matrix():
    r = lax.broadcasted_iota(jnp.int32, (256, 256), 0)
    c = lax.broadcasted_iota(jnp.int32, (256, 256), 1)
    return jnp.where(r == jnp.where(c < 128, 2 * c, 2 * c - 255), 1.0, 0.0).astype(jnp.bfloat16)


def join_matrix():
    r = lax.broadcasted_iota(jnp.int32, (256, 256), 0)
    c = lax.broadcasted_iota(jnp.int32, (256, 256), 1)
    return jnp.where(c == jnp.where(r < 128, 2 * r, 2 * r - 255), 1.0, 0.0).astype(jnp.bfloat16)


def parity_matrix():
    r = lax.broadcasted_iota(jnp.int32, (128, 128), 0)
    c = lax.broadcasted_iota(jnp.int32, (128, 128), 1)
    return jnp.where(r == jnp.where(c < 64, 2 * c, 2 * c - 127), 1.0, 0.0).astype(jnp.bfloat16)


def rows_of(x, zp, q):
    return pl.ds((4 * zp + 2 * (x // 8) + q) * 8 + x % 8, 8, stride=64)


def prepare(info, start, labels, s_out, m_out, outer, inner, s_in, l_in, rows, sems):
    core = info[0]
    copies = [pltpu.make_async_copy(labels, l_in, sems.at[3])]
    copies += [pltpu.make_async_copy(start.at[c], s_in.at[c], sems.at[c]) for c in range(3)]
    for copy in copies:
        copy.start()
    split = split_matrix()
    copies[0].wait()
    for x in range(NXB):
        for zp in (0, 1):
            for q in (0, 1):
                mobility = 1.0 / (1.0 + 3.0 * l_in[rows_of(x, zp, q), :].astype(F32))
                rows[3, pl.ds((x * 2 + zp) * 8, 8), 128 * q : 128 * q + 128] = mobility
    done = jnp.dot(rows[3].astype(jnp.bfloat16), split, preferred_element_type=F32)
    m_out[...] = done.reshape(NXB, 2, 8, 256)
    outer[pl.ds(3 * HS, HP)] = m_out[pl.ds((NXB - HP) * core, HP)]
    inner[pl.ds(3 * HS, HP)] = m_out[pl.ds((NXB - HP) * (1 - core), HP)]
    for c in range(3):
        copies[1 + c].wait()
        for x in range(NXB):
            for zp in (0, 1):
                for q in (0, 1):
                    rows[c, pl.ds((x * 2 + zp) * 8, 8), 128 * q : 128 * q + 128] = s_in[c, rows_of(x, zp, q), :]
        done = exact_dot(rows[c], split)
        s_out[c] = done.reshape(NXB, 2, 8, 256)
        outer[pl.ds(c * HS, HS)] = s_out[c, pl.ds((NXB - HS) * core, HS)]
        inner[pl.ds(c * HS, HS)] = s_out[c, pl.ds((NXB - HS) * (1 - core), HS)]


def interleave(base, nat):
    join = join_matrix()
    for c in range(3):
        done = exact_dot(base[c].reshape(256, 256), join)
        for x in range(NXB):
            for zp in (0, 1):
                at = (x * 2 + zp) * 8
                for q in (0, 1):
                    cols = slice(128 * q, 128 * q + 128)
                    nat[c, rows_of(x, zp, q), :] = done[at : at + 8, cols]


def finish(nat, w, out, made, sems):
    r = lax.broadcasted_iota(jnp.int32, (128, 256), 0)
    c = lax.broadcasted_iota(jnp.int32, (128, 256), 1)
    spread = jnp.where(lax.div(c, 2) == jnp.where(r < 64, 2 * r, 2 * r - 127), 1.0, 0.0).astype(jnp.bfloat16)
    done = exact_dot(w[...].reshape(192, 128), spread)
    copies = []
    for comp in range(3):
        for xc in range(NXB // 2):
            at = (comp * 8 + xc) * 8
            for q in (0, 1):
                cols = slice(128 * q, 128 * q + 128)
                value = done[at : at + 8, cols]
                for xp in (0, 1):
                    for zp in (0, 1):
                        sl = rows_of(2 * xc + xp, zp, q)
                        made[comp, sl, :] = nat[comp, sl, :] + value
        copies.append(pltpu.make_async_copy(made.at[comp], out.at[comp], sems.at[comp]))
        copies[-1].start()
    for copy in copies:
        copy.wait()


def valid_of(info):
    left, right = info[1].astype(F32), info[2].astype(F32)
    return lambda i, halo: jnp.where(i < halo, left, jnp.where(i >= halo + NXB, right, jnp.float32(1.0)))


def weigh(valid, mw, wt, dg, inv, mc, cw, cinv, fix, inside):
    def layer(i):
        m = quad(mw, i)
        sides = near(m, fix) + (quad(mw, i + 1), quad(mw, i - 1))
        ok = valid(i, HP)
        for zp, yp in QUAD:
            faces = [0.5 * (m[zp][yp] + s[zp][yp]) for s in sides]
            total = faces[0] + faces[1] + faces[2] + faces[3] + faces[4] + faces[5]
            if zp == 1:
                faces[0] = fix.zu(faces[0])
            else:
                faces[1] = fix.zd(faces[1])
            if yp == 1:
                faces[2] = fix.yu(faces[2])
            else:
                faces[3] = fix.yd(faces[3])
            for f in range(6):
                put(wt, (f, i), zp, yp, faces[f])
            put(dg, (i,), zp, yp, total)
            put(inv, (i,), zp, yp, (0.8 * ok) / (total + (1.0 - ok)))

    if inside:
        loop(HP + 1, HP + NXB - 1, layer, 7)
    else:
        loop(1, HP + 1, layer)
        loop(HP + NXB - 1, WN - 1, layer)

    def coarse(j):
        mc[j] = 0.125 * eight(mw, 2 * j)

    mine = range(HP // 2, HP // 2 + NXB // 2)
    for j in range(CN):
        if (j in mine) == inside:
            coarse(j)

    def coarse_layer(j):
        m = mc[j]
        sides = coarse_near(m, fix) + (mc[j + 1], mc[j - 1])
        ok = valid(2 * j, HP)
        faces = [0.125 * (m + s) for s in sides]
        total = faces[0] + faces[1] + faces[2] + faces[3] + faces[4] + faces[5]
        faces[0] = fix.zu(faces[0])
        faces[1] = fix.zd(faces[1])
        faces[2] = fix.yu(faces[2])
        faces[3] = fix.yd(faces[3])
        for f in range(6):
            cw[f, j] = faces[f]
        cinv[j] = (0.8 * ok) / (total + (1.0 - ok))

    mine = range(HP // 2 + 1, HP // 2 + NXB // 2 - 1)
    for j in range(1, CN - 1):
        if (j in mine) == inside:
            coarse_layer(j)


def predicting(valid, mw, sw, at, pr, fix):
    def predict(i):
        ok = valid(i, HP)
        m = quad(mw, i)
        for c in range(3):
            v = quad(sw, c, i + 1 - at)
            sides = near(v, fix) + (quad(sw, c, i + 2 - at), quad(sw, c, i - at))
            for zp, yp in QUAD:
                n = [s[zp][yp] for s in sides]
                total = ((n[0] + n[1]) + (n[2] + n[3])) + (n[4] + n[5])
                value = 0.4 * v[zp][yp] + 0.1 * total
                if c == 0:
                    value = value + (0.4 * m[zp][yp] - 0.2)
                put(pr, (c, i), zp, yp, ok * value)

    return predict


def gathered(p, i, wt):
    v = quad(p, i)
    sides = raw_near(v) + (quad(p, i + 1), quad(p, i - 1))
    ws = [quad(wt, f, i) for f in range(6)]
    total = [[None, None], [None, None]]
    for zp, yp in QUAD:
        terms = [ws[f][zp][yp] * sides[f][zp][yp] for f in range(6)]
        total[zp][yp] = ((terms[0] + terms[1]) + (terms[2] + terms[3])) + (terms[4] + terms[5])
    return v, total


def smooth(lo, hi, p, q, tw, wt, inv):
    def layer(i):
        v, total = gathered(p, i, wt)
        t, n = quad(tw, i), quad(inv, i)
        for zp, yp in QUAD:
            put(q, (i,), zp, yp, 0.2 * v[zp][yp] + n[zp][yp] * (t[zp][yp] + total[zp][yp]))

    loop(lo, hi, layer, (hi - lo) // 2)


def correct(p, tw, wt, dg, lo, ca, cb, cw, cinv):
    def coarse(j):
        out = None
        for i in (2 * j, 2 * j + 1):
            v, total = gathered(p, i, wt)
            t, d = quad(tw, i), quad(dg, i)
            for zp, yp in QUAD:
                r = (t[zp][yp] + total[zp][yp]) - d[zp][yp] * v[zp][yp]
                out = r if out is None else out + r
        out = 0.125 * out
        lo[j] = out
        ca[j] = cinv[j] * out

    loop(1, CN - 1, coarse, 8)

    def sweep(first, last, a, b):
        def layer(j):
            v = a[j]
            sides = (
                pltpu.roll(v, 7, 0),
                pltpu.roll(v, 1, 0),
                pltpu.roll(v, 127, 1),
                pltpu.roll(v, 1, 1),
                a[j + 1],
                a[j - 1],
            )
            terms = [cw[f, j] * sides[f] for f in range(6)]
            total = ((terms[0] + terms[1]) + (terms[2] + terms[3])) + (terms[4] + terms[5])
            b[j] = 0.2 * v + cinv[j] * (lo[j] + total)

        loop(first, last, layer)

    sweep(2, CN - 2, ca, cb)
    sweep(3, CN - 3, cb, ca)
    sweep(4, CN - 4, ca, cb)

    def add(j):
        g = cb[j]
        for i in (2 * j, 2 * j + 1):
            v = quad(p, i)
            for zp, yp in QUAD:
                put(p, (i,), zp, yp, v[zp][yp] + g)

    loop(4, CN - 4, add)


def inside(info, s_own, m_own, mw, wt, dg, inv, mc, cw, cinv, pr):
    fix = Fix()
    valid = valid_of(info)
    mw[pl.ds(HP, NXB)] = m_own[...]
    weigh(valid, mw, wt, dg, inv, mc, cw, cinv, fix, True)
    loop(HP + 1, HP + NXB - 1, predicting(valid, mw, s_own, HS, pr, fix), 7)


def first_cycle(info, s_own, off, on, *refs):
    mw, wt, dg, inv, mc, cw, cinv, pr, pred, tw, p1, outer, inner, gs, sw, p, lo, ca, cb, rs, rt = refs[8:]
    fix = Fix()
    core = info[0]
    valid = valid_of(info)
    off_s, on_s = core * (HS + NXB), (1 - core) * (HS + NXB)
    for c in range(3):
        sw[c, pl.ds(HS, NXB)] = s_own[c]
        sw[c, pl.ds(off_s, HS)] = off[pl.ds(c * HS, HS)]
        sw[c, pl.ds(on_s, HS)] = on[pl.ds(c * HS, HS)]
    mw[pl.ds(core * (HP + NXB), HP)] = off[pl.ds(3 * HS, HP)]
    mw[pl.ds((1 - core) * (HP + NXB), HP)] = on[pl.ds(3 * HS, HP)]
    weigh(valid, mw, wt, dg, inv, mc, cw, cinv, fix, False)
    predict = predicting(valid, mw, sw, 0, pr, fix)
    loop(0, HP + 1, predict)
    loop(HP + NXB - 1, WN, predict)

    def aim(i):
        a, b = quad(pr, 0, i), quad(pr, 2, i)
        zu, zd = z_up(a, fix.zu), z_down(a, fix.zd)
        yu, yd = y_up(b, fix.yu), y_down(b, fix.yd)
        xu, xd = quad(pr, 1, i + 1), quad(pr, 1, i - 1)
        n = quad(inv, i)
        for zp, yp in QUAD:
            t = (zu[zp][yp] - zd[zp][yp]) + (xu[zp][yp] - xd[zp][yp])
            t = -0.5 * (t + (yu[zp][yp] - yd[zp][yp]))
            put(tw, (i,), zp, yp, t)
            put(p, (i,), zp, yp, n[zp][yp] * t)

    loop(1, WN - 1, aim, 17)
    for c in range(3):
        pred[c] = pr[c, pl.ds(HP, NXB)]

    correct(p, tw, wt, dg, lo, ca, cb, cw, cinv)

    def last(x):
        i = x + HP
        v, total = gathered(p, i, wt)
        t, n = quad(tw, i), quad(inv, i)
        for zp, yp in QUAD:
            put(p1, (x,), zp, yp, 0.2 * v[zp][yp] + n[zp][yp] * (t[zp][yp] + total[zp][yp]))

    loop(0, NXB, last, 8)
    outer[...] = p1[pl.ds((NXB - HP) * core, HP)]
    inner[...] = p1[pl.ds((NXB - HP) * (1 - core), HP)]

    later = info[3].astype(F32)

    def shrink(q):
        for c in range(3):
            rs[c, q] = 0.125 * eight(sw.at[c], 2 * q + 7)

    loop(0, 12, shrink)

    def coarse_step(a, b, scale):
        def layer(q):
            m = mc[q + 3]
            for c in range(3):
                v = a[c, q]
                n = coarse_near(v, fix) + (a[c, q + 1], a[c, q - 1])
                total = ((n[0] + n[1]) + (n[2] + n[3])) + (n[4] + n[5])
                b(c, q, scale * ((1.0 - 0.9 * m) * v + (0.15 * m) * total))

        return layer

    def to_rt(c, q, value):
        rt[c, q] = value

    def to_gs(c, q, value):
        gs[c, q - 2] = value

    loop(1, 11, coarse_step(rs, to_rt, 1.0))
    loop(2, 10, coarse_step(rt, to_gs, later))


def second_cycle(info, pred, tw, p1, off, on, gs, mw, wt, dg, inv, mc, cw, cinv, base, send, p, q, lo, ca, cb, plain):
    fix = Fix()
    core, row = info[0], info[4]
    p[pl.ds(HP, NXB)] = p1[...]
    p[pl.ds(core * (HP + NXB), HP)] = off[...]
    p[pl.ds((1 - core) * (HP + NXB), HP)] = on[...]
    smooth(1, WN - 1, p, q, tw, wt, inv)
    correct(q, tw, wt, dg, lo, ca, cb, cw, cinv)
    smooth(HP - 1, HP + NXB + 1, q, p, tw, wt, inv)

    def finish_pair(j):
        sums = [None, None, None]
        held = []
        for i in (2 * j, 2 * j + 1):
            v = quad(p, i + HP)
            sides = near(v, fix)
            xu, xd = quad(p, i + HP + 1), quad(p, i + HP - 1)
            m = quad(mw, i + HP)
            up = (sides[0], xu, sides[2])
            down = (sides[1], xd, sides[3])
            for c in range(3):
                a = quad(pred, c, i)
                for zp, yp in QUAD:
                    e = a[zp][yp] - (0.5 * m[zp][yp]) * (up[c][zp][yp] - down[c][zp][yp])
                    held.append((c, i, zp, yp, e))
                    sums[c] = e if sums[c] is None else sums[c] + e
        means = [0.125 * s for s in sums]
        for c, i, zp, yp, e in held:
            put(base, (c, i), zp, yp, e - means[c])
        for c in range(3):
            plain[pl.ds((c * 8 + j) * 8, 8), :] = means[c] - gs[c, j]

    loop(0, NXB // 2, finish_pair, 4)
    for j in range(NXB // 2):
        plain[192 + 8 * j : 200 + 8 * j, :] = mc[HP // 2 + j]
    packed = exact_dot(plain[...], parity_matrix())
    plain[...] = packed
    for half in (0, 1):
        g = plain[pl.ds(192 + 8 * (4 * half + row), 8), :]
        for chip in range(4):
            for l in range(4):
                at = (min(chip, 2) * 8 + 4 * half + l) * 8
                for to in range(4):
                    send[to, chip, half, l] = packed[at : at + 8, :]
            for to in range(4):
                send[to, chip, half, 4] = g


NC = 64
PAD = 9
ROWS = 592


def at_layer(i, off=0):
    return pl.ds(PAD * i + 1 + off, 8)


class Pack:
    def __init__(self):
        j = iota(1)
        self.low = j < 64
        self.not_first = lax.rem(j, 64) > 0
        self.not_last = lax.rem(j, 64) < 63

    def join(self, one, two):
        return jnp.where(self.low, one, pltpu.roll(two, 64, 1)), jnp.where(self.low, pltpu.roll(one, 64, 1), two)


def substep(a, b, wa, wb, pack, begin):
    held = {}

    def pair(i):
        if i not in held:
            held[i] = (a[at_layer(i), :], a[at_layer(32 + i), :])
        return held[i]

    def ends(i, keep_low):
        zero = jnp.zeros((8, 128), F32)
        out = []
        for odd in (0, 1):
            r = pltpu.roll(a[at_layer(32 * odd + i), :], 64, 1)
            out.append(jnp.where(pack.low, r, zero) if keep_low else jnp.where(pack.low, zero, r))
        return out

    for n in range(32):
        i = (begin + n) % 32
        here = pair(i)
        down = pair(i - 1) if i > 0 else ends(31, False)
        up = pair(i + 1) if i < 31 else ends(0, True)
        sides = (
            jnp.where(pack.not_first, pltpu.roll(here[1], 1, 1), 0.0),
            jnp.where(pack.not_last, pltpu.roll(here[0], 127, 1), 0.0),
        )
        for odd in (0, 1):
            at = 32 * odd + i
            total = (a[at_layer(at, 1), :] + a[at_layer(at, -1), :]) + (up[odd] + down[odd])
            total = total + (here[1 - odd] + sides[odd])
            b[at_layer(at), :] = wa[at] * here[odd] + wb[at] * total
        held.pop(i - 1, None)


def advance(times, a, b, wa, wb, pack):
    each = 4 if times % 4 == 0 else times

    def turn(t, carry):
        for k in range(each):
            substep(a, b, wa, wb, pack, 4 * k)
            substep(b, a, wa, wb, pack, 4 * k + 2)
        return carry

    if times == each:
        turn(0, 0)
    else:
        lax.fori_loop(0, times // each, turn, 0)


def take_half(half, src, core):
    for odd in (0, 1):
        half[16 * odd : 16 * odd + 16] = src[pl.ds(32 * odd + 16 * core, 16)]


def rows_scan(info, got, swapped, acc, half, wa, wb, a, b):
    pack = Pack()
    core, row = info[0], info[4]
    a[...] = jnp.zeros_like(a)
    b[...] = jnp.zeros_like(b)

    def each(fn):
        for s in range(4):
            for l in range(4):
                for part, src in ((core, got), (1 - core, swapped)):
                    fn(s, l, 8 * s + 4 * part + l, src)

    def begin(s, l, at, src):
        even, odd = pack.join(src[l, s, 4], src[l, s + 4, 4])
        for base, m in ((0, even), (32, odd)):
            wa[base + at] = 1.0 - 0.9 * m
            wb[base + at] = 0.15 * m
        even, odd = pack.join(src[0, s, l], src[0, s + 4, l])
        a[at_layer(at), :] = even
        a[at_layer(32 + at), :] = odd

    each(begin)
    for t in range(1, 4):

        @pl.when(t <= row)
        def _():
            advance(8, a, b, wa, wb, pack)

            def include(s, l, at, src):
                even, odd = pack.join(src[t, s, l], src[t, s + 4, l])
                a[at_layer(at), :] = a[at_layer(at), :] + even
                a[at_layer(32 + at), :] = a[at_layer(32 + at), :] + odd

            each(include)

    for i in range(NC):
        acc[i] = a[at_layer(i), :]
    take_half(half, acc, core)


def load_halves(a, own, other, core, add):
    for odd in (0, 1):
        for i in range(16):
            for part, src in ((core, own), (1 - core, other)):
                at = at_layer(32 * odd + 16 * part + i)
                value = src[16 * odd + i]
                a[at, :] = a[at, :] + value if add else value


def one_scan(info, acc, own, other, wa, wb, out, half, a, b):
    pack = Pack()
    core = info[0]
    a[...] = jnp.zeros_like(a)
    b[...] = jnp.zeros_like(b)
    load_halves(a, own, other, core, False)
    advance(1, a, b, wa, wb, pack)
    for i in range(NC):
        out[i] = acc[i] + a[at_layer(i), :]
    take_half(half, out, core)


def even_scan(info, acc, own, other, wa, wb, chunk, out, a, b):
    pack = Pack()
    core = info[0]
    a[...] = jnp.zeros_like(a)
    b[...] = jnp.zeros_like(b)
    load_halves(a, own.at[2], other.at[2], core, False)
    advance(2, a, b, wa, wb, pack)
    load_halves(a, own.at[1], other.at[1], core, True)
    advance(2, a, b, wa, wb, pack)
    load_halves(a, own.at[0], other.at[0], core, True)
    advance(2, a, b, wa, wb, pack)
    for i in range(NC):
        out[i] = acc[i] + a[at_layer(i), :]
    for s in range(4):
        for l in range(4):
            at = 8 * s + 4 * core + l
            one, two = pack.join(out[at], out[32 + at])
            chunk[s, l] = one
            chunk[s + 4, l] = two


def tiles(a):
    return a.reshape(-1, 32, 8, 2, 128).transpose(0, 1, 3, 2, 4).reshape(-1, 512, 128)


def body(ny, nz, start_states, labels):
    ns = lax.axis_size("space")
    s = lax.axis_index("space")
    y = lax.axis_index("y")
    quarter = lax.axis_index("zq")
    z = 2 * quarter + lax.axis_index("zp")
    core = lax.rem(s, 2)
    info = jnp.stack([core, s > 0, s < ns - 1, y * nz + z > 0, y, quarter, s, s]).astype(jnp.int32)
    swap = [(i, i ^ 1) for i in range(ns)]
    cross = [(i, i + 1) for i in range(1, ns - 1, 2)]
    cross = cross + [(b, a) for a, b in cross]

    def exchange(outer, inner):
        off = lax.ppermute(outer, "space", cross)
        on = lax.ppermute(inner, "space", swap)
        return off, on

    start = tiles(start_states.reshape(3, 512, 128))
    label = tiles(labels.reshape(1, 16 * NXB, 256))[0]
    layer = (2, 8, 256)
    vm = lambda *d: pltpu.VMEM(d, F32)
    window = shape(WN, *layer)
    edge = shape(HP, *layer)
    both = shape(3 * HS + HP, *layer)
    s_own, m_own, outer, inner = call(
        prepare,
        [shape(3, NXB, *layer), shape(NXB, *layer), both, both],
        [info, pltpu.with_memory_space_constraint(start, pltpu.HBM), pltpu.with_memory_space_constraint(label, pltpu.HBM)],
        [vm(3, 512, 128), pltpu.VMEM((512, 128), jnp.int32), vm(4, 256, 256), pltpu.SemaphoreType.DMA((4,))],
        ANY,
    )
    off, on = exchange(outer, inner)
    kept = [window, shape(6, WN, *layer), window, window, shape(CN, 8, 128), shape(6, CN, 8, 128), shape(CN, 8, 128)]
    kept.append(shape(3, WN, *layer))
    held = call(inside, kept, [info, s_own, m_own])
    coarse = [vm(CN, 8, 128)] * 3
    done = call(
        first_cycle,
        kept + [shape(3, NXB, *layer), window, shape(NXB, *layer), edge, edge, shape(3, 8, 8, 128)],
        [info, s_own, off, on] + list(held),
        [vm(3, NXB + 2 * HS, *layer), vm(WN, *layer)] + coarse + [vm(3, 12, 8, 128)] * 2,
        aliases={4 + i: i for i in range(8)},
    )
    held, (pred, tw, p1, outer, inner, gs) = done[:7], done[8:]
    off, on = exchange(outer, inner)
    base, send = call(
        second_cycle,
        [shape(3, NXB, *layer), shape(4, 4, 2, 5, 8, 128)],
        [info, pred, tw, p1, off, on, gs] + list(held),
        [vm(WN, *layer)] * 2 + coarse + [vm(256, 128)],
    )
    got = lax.all_to_all(send.reshape(ny * ns, 5, 8, 128), ("y", "space"), 0, 0)
    got = got.reshape(ny, ns, 5, 8, 128)
    swapped = lax.ppermute(got, "space", swap)
    acc, half, wa, wb = call(
        rows_scan,
        [shape(NC, 8, 128), shape(NC // 2, 8, 128), shape(NC, 8, 128), shape(NC, 8, 128)],
        [info, got, swapped],
        [vm(ROWS, 128)] * 2,
    )
    nt = ny * nz

    def shifted(value, k):
        return lax.ppermute(value, ("y", "zq", "zp"), [(i, i + k) for i in range(nt - k)])

    own = shifted(half, 1)
    other = lax.ppermute(own, "space", swap)
    state = [vm(ROWS, 128)] * 2
    acc, half = call(
        one_scan, [shape(NC, 8, 128), shape(NC // 2, 8, 128)], [info, acc, own, other, wa, wb], state
    )
    own = jnp.stack([shifted(half, k) for k in (2, 4, 6)])
    other = lax.ppermute(own, "space", swap)
    (chunks,) = call(
        even_scan, [shape(8, 4, 8, 128)], [info, acc, own, other, wa, wb], [vm(NC, 8, 128)] + state
    )
    (nat,) = call(interleave, [shape(3, 512, 128)], [base])
    back = lax.all_to_all(chunks, "space", 0, 0)
    w = back[:6].reshape(3, 8, 8, 128)
    (out,) = call(finish, [shape(3, 512, 128)], [nat, w], [vm(3, 512, 128), pltpu.SemaphoreType.DMA((3,))], VM, ANY)
    out = out.reshape(3, 32, 2, 8, 128).transpose(0, 1, 3, 2, 4)
    return out.reshape(1, 3, 16, NXB, 256)


def solution(mesh):
    nz = 8
    ny = mesh.shape["tm"] // nz
    split = Mesh(mesh.devices.reshape(ny, nz // 2, 2, mesh.shape["space"]), ("y", "zq", "zp", "space"))
    in_specs = (P(("y", "zq", "zp"), None, None, "space", None), P(None, "space", None))
    out_specs = P(("y", "zq", "zp"), None, None, "space", None)

    def run(start_states, labels):
        return body(ny, nz, start_states, labels)

    return jax.shard_map(run, mesh=split, in_specs=in_specs, out_specs=out_specs, check_vma=False)
```

```python
import jax
import jax.numpy as jnp
from jax import lax
from jax.experimental import pallas as pl
from jax.experimental.pallas import tpu as pltpu
from jax.sharding import Mesh, PartitionSpec as P

F32 = jnp.float32
VM = pl.BlockSpec(memory_space=pltpu.VMEM)
SM = pl.BlockSpec(memory_space=pltpu.SMEM)
ANY = pl.BlockSpec(memory_space=pltpu.HBM)

NXB = 16
HS = 11
HP = 10
WN = NXB + 2 * HP
CN = WN // 2


def shape(*dims):
    return jax.ShapeDtypeStruct(dims, F32)


def call(kernel, outs, ins, scratch=(), where=VM, to=VM, aliases={}):
    specs = [SM if a.dtype == jnp.int32 and a.ndim == 1 else where for a in ins]
    moved = sum(a.size * 4 for a in ins) + sum(4 * _size(o) for o in outs)
    return pl.pallas_call(
        kernel,
        out_shape=outs,
        in_specs=specs,
        out_specs=[to] * len(outs),
        scratch_shapes=list(scratch),
        input_output_aliases=aliases,
        compiler_params=pltpu.CompilerParams(vmem_limit_bytes=28 * 1024 * 1024),
        cost_estimate=pl.CostEstimate(flops=1000000, bytes_accessed=moved, transcendentals=0),
    )(*ins)


def _size(o):
    n = 1
    for d in o.shape:
        n *= d
    return n


def loop(lo, hi, fn, unroll=0):
    unroll = unroll or hi - lo
    if unroll == hi - lo:
        for i in range(lo, hi):
            fn(i)
        return
    assert (hi - lo) % unroll == 0

    def step(t, carry):
        for u in range(unroll):
            fn(lo + t * unroll + u)
        return carry

    lax.fori_loop(0, (hi - lo) // unroll, step, 0)


def iota(dim):
    return lax.broadcasted_iota(jnp.int32, (8, 128), dim)


def quad(ref, *at):
    return [[ref[(*at, zp, slice(None), slice(128 * yp, 128 * yp + 128))] for yp in (0, 1)] for zp in (0, 1)]


def put(ref, at, zp, yp, value):
    ref[(*at, zp, slice(None), slice(128 * yp, 128 * yp + 128))] = value


def z_up(v, fix=None):
    f = fix or (lambda r: r)
    return [v[1], [f(pltpu.roll(v[0][q], 7, 0)) for q in (0, 1)]]


def z_down(v, fix=None):
    f = fix or (lambda r: r)
    return [[f(pltpu.roll(v[1][q], 1, 0)) for q in (0, 1)], v[0]]


def y_up(v, fix=None):
    f = fix or (lambda r: r)
    return [[v[q][1], f(pltpu.roll(v[q][0], 127, 1))] for q in (0, 1)]


def y_down(v, fix=None):
    f = fix or (lambda r: r)
    return [[f(pltpu.roll(v[q][1], 1, 1)), v[q][0]] for q in (0, 1)]


class Fix:
    def __init__(self):
        k, j = iota(0), iota(1)
        self.zu = lambda r: jnp.where(k < 7, r, 0.0)
        self.zd = lambda r: jnp.where(k > 0, r, 0.0)
        self.yu = lambda r: jnp.where(j < 127, r, 0.0)
        self.yd = lambda r: jnp.where(j > 0, r, 0.0)


def coarse_near(v, fix):
    return (
        fix.zu(pltpu.roll(v, 7, 0)),
        fix.zd(pltpu.roll(v, 1, 0)),
        fix.yu(pltpu.roll(v, 127, 1)),
        fix.yd(pltpu.roll(v, 1, 1)),
    )


def near(v, fix):
    return (z_up(v, fix.zu), z_down(v, fix.zd), y_up(v, fix.yu), y_down(v, fix.yd))


def raw_near(v):
    return (z_up(v), z_down(v), y_up(v), y_down(v))


QUAD = [(zp, yp) for zp in (0, 1) for yp in (0, 1)]


def eight(ref, i):
    total = None
    for layer in (i, i + 1):
        v = quad(ref, layer)
        for zp, yp in QUAD:
            total = v[zp][yp] if total is None else total + v[zp][yp]
    return total


def exact_dot(x, chooser):
    one = x.astype(jnp.bfloat16)
    rest = x - one.astype(F32)
    two = rest.astype(jnp.bfloat16)
    three = (rest - two.astype(F32)).astype(jnp.bfloat16)
    dot = lambda part: jnp.dot(part, chooser, preferred_element_type=F32)
    return (dot(three) + dot(two)) + dot(one)


def split_matrix():
    r = lax.broadcasted_iota(jnp.int32, (256, 256), 0)
    c = lax.broadcasted_iota(jnp.int32, (256, 256), 1)
    return jnp.where(r == jnp.where(c < 128, 2 * c, 2 * c - 255), 1.0, 0.0).astype(jnp.bfloat16)


def join_matrix():
    r = lax.broadcasted_iota(jnp.int32, (256, 256), 0)
    c = lax.broadcasted_iota(jnp.int32, (256, 256), 1)
    return jnp.where(c == jnp.where(r < 128, 2 * r, 2 * r - 255), 1.0, 0.0).astype(jnp.bfloat16)


def parity_matrix():
    r = lax.broadcasted_iota(jnp.int32, (128, 128), 0)
    c = lax.broadcasted_iota(jnp.int32, (128, 128), 1)
    return jnp.where(r == jnp.where(c < 64, 2 * c, 2 * c - 127), 1.0, 0.0).astype(jnp.bfloat16)


def rows_of(x, zp, q):
    return pl.ds((4 * zp + 2 * (x // 8) + q) * 8 + x % 8, 8, stride=64)


def prepare(info, start, labels, s_out, m_out, outer, inner, s_in, l_in, rows, sems):
    core = info[0]
    copies = [pltpu.make_async_copy(labels, l_in, sems.at[3])]
    copies += [pltpu.make_async_copy(start.at[c], s_in.at[c], sems.at[c]) for c in range(3)]
    for copy in copies:
        copy.start()
    split = split_matrix()
    copies[0].wait()
    for x in range(NXB):
        for zp in (0, 1):
            for q in (0, 1):
                mobility = 1.0 / (1.0 + 3.0 * l_in[rows_of(x, zp, q), :].astype(F32))
                rows[3, pl.ds((x * 2 + zp) * 8, 8), 128 * q : 128 * q + 128] = mobility
    done = jnp.dot(rows[3].astype(jnp.bfloat16), split, preferred_element_type=F32)
    m_out[...] = done.reshape(NXB, 2, 8, 256)
    outer[pl.ds(3 * HS, HP)] = m_out[pl.ds((NXB - HP) * core, HP)]
    inner[pl.ds(3 * HS, HP)] = m_out[pl.ds((NXB - HP) * (1 - core), HP)]
    for c in range(3):
        copies[1 + c].wait()
        for x in range(NXB):
            for zp in (0, 1):
                for q in (0, 1):
                    rows[c, pl.ds((x * 2 + zp) * 8, 8), 128 * q : 128 * q + 128] = s_in[c, rows_of(x, zp, q), :]
        done = exact_dot(rows[c], split)
        s_out[c] = done.reshape(NXB, 2, 8, 256)
        outer[pl.ds(c * HS, HS)] = s_out[c, pl.ds((NXB - HS) * core, HS)]
        inner[pl.ds(c * HS, HS)] = s_out[c, pl.ds((NXB - HS) * (1 - core), HS)]


def interleave(base, nat):
    join = join_matrix()
    for c in range(3):
        done = exact_dot(base[c].reshape(256, 256), join)
        for x in range(NXB):
            for zp in (0, 1):
                at = (x * 2 + zp) * 8
                for q in (0, 1):
                    cols = slice(128 * q, 128 * q + 128)
                    nat[c, rows_of(x, zp, q), :] = done[at : at + 8, cols]


def finish(nat, w, out, made, sems):
    r = lax.broadcasted_iota(jnp.int32, (128, 256), 0)
    c = lax.broadcasted_iota(jnp.int32, (128, 256), 1)
    spread = jnp.where(lax.div(c, 2) == jnp.where(r < 64, 2 * r, 2 * r - 127), 1.0, 0.0).astype(jnp.bfloat16)
    done = exact_dot(w[...].reshape(192, 128), spread)
    copies = []
    for comp in range(3):
        for xc in range(NXB // 2):
            at = (comp * 8 + xc) * 8
            for q in (0, 1):
                cols = slice(128 * q, 128 * q + 128)
                value = done[at : at + 8, cols]
                for xp in (0, 1):
                    for zp in (0, 1):
                        sl = rows_of(2 * xc + xp, zp, q)
                        made[comp, sl, :] = nat[comp, sl, :] + value
        copies.append(pltpu.make_async_copy(made.at[comp], out.at[comp], sems.at[comp]))
        copies[-1].start()
    for copy in copies:
        copy.wait()


def valid_of(info):
    left, right = info[1].astype(F32), info[2].astype(F32)
    return lambda i, halo: jnp.where(i < halo, left, jnp.where(i >= halo + NXB, right, jnp.float32(1.0)))


def weigh(valid, mw, wt, dg, inv, mc, cw, cinv, fix, inside):
    def layer(i):
        m = quad(mw, i)
        sides = near(m, fix) + (quad(mw, i + 1), quad(mw, i - 1))
        ok = valid(i, HP)
        for zp, yp in QUAD:
            faces = [0.5 * (m[zp][yp] + s[zp][yp]) for s in sides]
            total = faces[0] + faces[1] + faces[2] + faces[3] + faces[4] + faces[5]
            if zp == 1:
                faces[0] = fix.zu(faces[0])
            else:
                faces[1] = fix.zd(faces[1])
            if yp == 1:
                faces[2] = fix.yu(faces[2])
            else:
                faces[3] = fix.yd(faces[3])
            for f in range(6):
                put(wt, (f, i), zp, yp, faces[f])
            put(dg, (i,), zp, yp, total)
            put(inv, (i,), zp, yp, (0.8 * ok) / (total + (1.0 - ok)))

    if inside:
        loop(HP + 1, HP + NXB - 1, layer, 7)
    else:
        loop(1, HP + 1, layer)
        loop(HP + NXB - 1, WN - 1, layer)

    def coarse(j):
        mc[j] = 0.125 * eight(mw, 2 * j)

    mine = range(HP // 2, HP // 2 + NXB // 2)
    for j in range(CN):
        if (j in mine) == inside:
            coarse(j)

    def coarse_layer(j):
        m = mc[j]
        sides = coarse_near(m, fix) + (mc[j + 1], mc[j - 1])
        ok = valid(2 * j, HP)
        faces = [0.125 * (m + s) for s in sides]
        total = faces[0] + faces[1] + faces[2] + faces[3] + faces[4] + faces[5]
        faces[0] = fix.zu(faces[0])
        faces[1] = fix.zd(faces[1])
        faces[2] = fix.yu(faces[2])
        faces[3] = fix.yd(faces[3])
        for f in range(6):
            cw[f, j] = faces[f]
        cinv[j] = (0.8 * ok) / (total + (1.0 - ok))

    mine = range(HP // 2 + 1, HP // 2 + NXB // 2 - 1)
    for j in range(1, CN - 1):
        if (j in mine) == inside:
            coarse_layer(j)


def predicting(valid, mw, sw, at, pr, fix):
    def predict(i):
        ok = valid(i, HP)
        m = quad(mw, i)
        for c in range(3):
            v = quad(sw, c, i + 1 - at)
            sides = near(v, fix) + (quad(sw, c, i + 2 - at), quad(sw, c, i - at))
            for zp, yp in QUAD:
                n = [s[zp][yp] for s in sides]
                total = ((n[0] + n[1]) + (n[2] + n[3])) + (n[4] + n[5])
                value = 0.4 * v[zp][yp] + 0.1 * total
                if c == 0:
                    value = value + (0.4 * m[zp][yp] - 0.2)
                put(pr, (c, i), zp, yp, ok * value)

    return predict


def gathered(p, i, wt):
    v = quad(p, i)
    sides = raw_near(v) + (quad(p, i + 1), quad(p, i - 1))
    ws = [quad(wt, f, i) for f in range(6)]
    total = [[None, None], [None, None]]
    for zp, yp in QUAD:
        terms = [ws[f][zp][yp] * sides[f][zp][yp] for f in range(6)]
        total[zp][yp] = ((terms[0] + terms[1]) + (terms[2] + terms[3])) + (terms[4] + terms[5])
    return v, total


def smooth(lo, hi, p, q, tw, wt, inv):
    def layer(i):
        v, total = gathered(p, i, wt)
        t, n = quad(tw, i), quad(inv, i)
        for zp, yp in QUAD:
            put(q, (i,), zp, yp, 0.2 * v[zp][yp] + n[zp][yp] * (t[zp][yp] + total[zp][yp]))

    loop(lo, hi, layer, (hi - lo) // 2)


def correct(p, tw, wt, dg, lo, ca, cb, cw, cinv):
    def coarse(j):
        out = None
        for i in (2 * j, 2 * j + 1):
            v, total = gathered(p, i, wt)
            t, d = quad(tw, i), quad(dg, i)
            for zp, yp in QUAD:
                r = (t[zp][yp] + total[zp][yp]) - d[zp][yp] * v[zp][yp]
                out = r if out is None else out + r
        out = 0.125 * out
        lo[j] = out
        ca[j] = cinv[j] * out

    loop(1, CN - 1, coarse, 8)

    def sweep(first, last, a, b):
        def layer(j):
            v = a[j]
            sides = (
                pltpu.roll(v, 7, 0),
                pltpu.roll(v, 1, 0),
                pltpu.roll(v, 127, 1),
                pltpu.roll(v, 1, 1),
                a[j + 1],
                a[j - 1],
            )
            terms = [cw[f, j] * sides[f] for f in range(6)]
            total = ((terms[0] + terms[1]) + (terms[2] + terms[3])) + (terms[4] + terms[5])
            b[j] = 0.2 * v + cinv[j] * (lo[j] + total)

        loop(first, last, layer)

    sweep(2, CN - 2, ca, cb)
    sweep(3, CN - 3, cb, ca)
    sweep(4, CN - 4, ca, cb)

    def add(j):
        g = cb[j]
        for i in (2 * j, 2 * j + 1):
            v = quad(p, i)
            for zp, yp in QUAD:
                put(p, (i,), zp, yp, v[zp][yp] + g)

    loop(4, CN - 4, add)


def inside(info, s_own, m_own, mw, wt, dg, inv, mc, cw, cinv, pr):
    fix = Fix()
    valid = valid_of(info)
    mw[pl.ds(HP, NXB)] = m_own[...]
    weigh(valid, mw, wt, dg, inv, mc, cw, cinv, fix, True)
    loop(HP + 1, HP + NXB - 1, predicting(valid, mw, s_own, HS, pr, fix), 7)


def first_cycle(info, s_own, off, on, *refs):
    mw, wt, dg, inv, mc, cw, cinv, pr, pred, tw, p1, outer, inner, gs, sw, p, lo, ca, cb, rs, rt = refs[8:]
    fix = Fix()
    core = info[0]
    valid = valid_of(info)
    off_s, on_s = core * (HS + NXB), (1 - core) * (HS + NXB)
    for c in range(3):
        sw[c, pl.ds(HS, NXB)] = s_own[c]
        sw[c, pl.ds(off_s, HS)] = off[pl.ds(c * HS, HS)]
        sw[c, pl.ds(on_s, HS)] = on[pl.ds(c * HS, HS)]
    mw[pl.ds(core * (HP + NXB), HP)] = off[pl.ds(3 * HS, HP)]
    mw[pl.ds((1 - core) * (HP + NXB), HP)] = on[pl.ds(3 * HS, HP)]
    weigh(valid, mw, wt, dg, inv, mc, cw, cinv, fix, False)
    predict = predicting(valid, mw, sw, 0, pr, fix)
    loop(0, HP + 1, predict)
    loop(HP + NXB - 1, WN, predict)

    def aim(i):
        a, b = quad(pr, 0, i), quad(pr, 2, i)
        zu, zd = z_up(a, fix.zu), z_down(a, fix.zd)
        yu, yd = y_up(b, fix.yu), y_down(b, fix.yd)
        xu, xd = quad(pr, 1, i + 1), quad(pr, 1, i - 1)
        n = quad(inv, i)
        for zp, yp in QUAD:
            t = (zu[zp][yp] - zd[zp][yp]) + (xu[zp][yp] - xd[zp][yp])
            t = -0.5 * (t + (yu[zp][yp] - yd[zp][yp]))
            put(tw, (i,), zp, yp, t)
            put(p, (i,), zp, yp, n[zp][yp] * t)

    loop(1, WN - 1, aim, 17)
    for c in range(3):
        pred[c] = pr[c, pl.ds(HP, NXB)]

    correct(p, tw, wt, dg, lo, ca, cb, cw, cinv)

    def last(x):
        i = x + HP
        v, total = gathered(p, i, wt)
        t, n = quad(tw, i), quad(inv, i)
        for zp, yp in QUAD:
            put(p1, (x,), zp, yp, 0.2 * v[zp][yp] + n[zp][yp] * (t[zp][yp] + total[zp][yp]))

    loop(0, NXB, last, 8)
    outer[...] = p1[pl.ds((NXB - HP) * core, HP)]
    inner[...] = p1[pl.ds((NXB - HP) * (1 - core), HP)]

    later = info[3].astype(F32)

    def shrink(q):
        for c in range(3):
            rs[c, q] = 0.125 * eight(sw.at[c], 2 * q + 7)

    loop(0, 12, shrink)

    def coarse_step(a, b, scale):
        def layer(q):
            m = mc[q + 3]
            for c in range(3):
                v = a[c, q]
                n = coarse_near(v, fix) + (a[c, q + 1], a[c, q - 1])
                total = ((n[0] + n[1]) + (n[2] + n[3])) + (n[4] + n[5])
                b(c, q, scale * ((1.0 - 0.9 * m) * v + (0.15 * m) * total))

        return layer

    def to_rt(c, q, value):
        rt[c, q] = value

    def to_gs(c, q, value):
        gs[c, q - 2] = value

    loop(1, 11, coarse_step(rs, to_rt, 1.0))
    loop(2, 10, coarse_step(rt, to_gs, later))


def second_cycle(info, pred, tw, p1, off, on, gs, mw, wt, dg, inv, mc, cw, cinv, base, send, p, q, lo, ca, cb, plain):
    fix = Fix()
    core, row = info[0], info[4]
    p[pl.ds(HP, NXB)] = p1[...]
    p[pl.ds(core * (HP + NXB), HP)] = off[...]
    p[pl.ds((1 - core) * (HP + NXB), HP)] = on[...]
    smooth(1, WN - 1, p, q, tw, wt, inv)
    correct(q, tw, wt, dg, lo, ca, cb, cw, cinv)
    smooth(HP - 1, HP + NXB + 1, q, p, tw, wt, inv)

    def finish_pair(j):
        sums = [None, None, None]
        held = []
        for i in (2 * j, 2 * j + 1):
            v = quad(p, i + HP)
            sides = near(v, fix)
            xu, xd = quad(p, i + HP + 1), quad(p, i + HP - 1)
            m = quad(mw, i + HP)
            up = (sides[0], xu, sides[2])
            down = (sides[1], xd, sides[3])
            for c in range(3):
                a = quad(pred, c, i)
                for zp, yp in QUAD:
                    e = a[zp][yp] - (0.5 * m[zp][yp]) * (up[c][zp][yp] - down[c][zp][yp])
                    held.append((c, i, zp, yp, e))
                    sums[c] = e if sums[c] is None else sums[c] + e
        means = [0.125 * s for s in sums]
        for c, i, zp, yp, e in held:
            put(base, (c, i), zp, yp, e - means[c])
        for c in range(3):
            plain[pl.ds((c * 8 + j) * 8, 8), :] = means[c] - gs[c, j]

    loop(0, NXB // 2, finish_pair, 4)
    for j in range(NXB // 2):
        plain[192 + 8 * j : 200 + 8 * j, :] = mc[HP // 2 + j]
    packed = exact_dot(plain[...], parity_matrix())
    plain[...] = packed
    for half in (0, 1):
        g = plain[pl.ds(192 + 8 * (4 * half + row), 8), :]
        for chip in range(4):
            for l in range(4):
                at = (min(chip, 2) * 8 + 4 * half + l) * 8
                for to in range(4):
                    send[to, chip, half, l] = packed[at : at + 8, :]
            for to in range(4):
                send[to, chip, half, 4] = g


NC = 64
PAD = 9
ROWS = 592


def at_layer(i, off=0):
    return pl.ds(PAD * i + 1 + off, 8)


class Pack:
    def __init__(self):
        j = iota(1)
        self.low = j < 64
        self.not_first = lax.rem(j, 64) > 0
        self.not_last = lax.rem(j, 64) < 63

    def join(self, one, two):
        return jnp.where(self.low, one, pltpu.roll(two, 64, 1)), jnp.where(self.low, pltpu.roll(one, 64, 1), two)


def substep(a, b, wa, wb, pack, begin):
    held = {}

    def pair(i):
        if i not in held:
            held[i] = (a[at_layer(i), :], a[at_layer(32 + i), :])
        return held[i]

    def ends(i, keep_low):
        zero = jnp.zeros((8, 128), F32)
        out = []
        for odd in (0, 1):
            r = pltpu.roll(a[at_layer(32 * odd + i), :], 64, 1)
            out.append(jnp.where(pack.low, r, zero) if keep_low else jnp.where(pack.low, zero, r))
        return out

    for n in range(32):
        i = (begin + n) % 32
        here = pair(i)
        down = pair(i - 1) if i > 0 else ends(31, False)
        up = pair(i + 1) if i < 31 else ends(0, True)
        sides = (
            jnp.where(pack.not_first, pltpu.roll(here[1], 1, 1), 0.0),
            jnp.where(pack.not_last, pltpu.roll(here[0], 127, 1), 0.0),
        )
        for odd in (0, 1):
            at = 32 * odd + i
            total = (a[at_layer(at, 1), :] + a[at_layer(at, -1), :]) + (up[odd] + down[odd])
            total = total + (here[1 - odd] + sides[odd])
            b[at_layer(at), :] = wa[at] * here[odd] + wb[at] * total
        held.pop(i - 1, None)


def advance(times, a, b, wa, wb, pack):
    each = 4 if times % 4 == 0 else times

    def turn(t, carry):
        for k in range(each):
            substep(a, b, wa, wb, pack, 4 * k)
            substep(b, a, wa, wb, pack, 4 * k + 2)
        return carry

    if times == each:
        turn(0, 0)
    else:
        lax.fori_loop(0, times // each, turn, 0)


def take_half(half, src, core):
    for odd in (0, 1):
        half[16 * odd : 16 * odd + 16] = src[pl.ds(32 * odd + 16 * core, 16)]


def rows_scan(info, got, swapped, acc, half, wa, wb, a, b):
    pack = Pack()
    core, row = info[0], info[4]
    a[...] = jnp.zeros_like(a)
    b[...] = jnp.zeros_like(b)

    def each(fn):
        for s in range(4):
            for l in range(4):
                for part, src in ((core, got), (1 - core, swapped)):
                    fn(s, l, 8 * s + 4 * part + l, src)

    def begin(s, l, at, src):
        even, odd = pack.join(src[l, s, 4], src[l, s + 4, 4])
        for base, m in ((0, even), (32, odd)):
            wa[base + at] = 1.0 - 0.9 * m
            wb[base + at] = 0.15 * m
        even, odd = pack.join(src[0, s, l], src[0, s + 4, l])
        a[at_layer(at), :] = even
        a[at_layer(32 + at), :] = odd

    each(begin)
    for t in range(1, 4):

        @pl.when(t <= row)
        def _():
            advance(8, a, b, wa, wb, pack)

            def include(s, l, at, src):
                even, odd = pack.join(src[t, s, l], src[t, s + 4, l])
                a[at_layer(at), :] = a[at_layer(at), :] + even
                a[at_layer(32 + at), :] = a[at_layer(32 + at), :] + odd

            each(include)

    for i in range(NC):
        acc[i] = a[at_layer(i), :]
    take_half(half, acc, core)


def load_halves(a, own, other, core, add):
    for odd in (0, 1):
        for i in range(16):
            for part, src in ((core, own), (1 - core, other)):
                at = at_layer(32 * odd + 16 * part + i)
                value = src[16 * odd + i]
                a[at, :] = a[at, :] + value if add else value


def one_scan(info, acc, own, other, wa, wb, out, half, a, b):
    pack = Pack()
    core = info[0]
    a[...] = jnp.zeros_like(a)
    b[...] = jnp.zeros_like(b)
    load_halves(a, own, other, core, False)
    advance(1, a, b, wa, wb, pack)
    for i in range(NC):
        out[i] = acc[i] + a[at_layer(i), :]
    take_half(half, out, core)


def even_scan(info, acc, *refs):
    own, other = refs[:3], refs[3:6]
    wa, wb, chunk, out, a, b = refs[6:]
    pack = Pack()
    core = info[0]
    a[...] = jnp.zeros_like(a)
    b[...] = jnp.zeros_like(b)
    load_halves(a, own[2], other[2], core, False)
    advance(2, a, b, wa, wb, pack)
    load_halves(a, own[1], other[1], core, True)
    advance(2, a, b, wa, wb, pack)
    load_halves(a, own[0], other[0], core, True)
    advance(2, a, b, wa, wb, pack)
    for i in range(NC):
        out[i] = acc[i] + a[at_layer(i), :]
    for s in range(4):
        for l in range(4):
            at = 8 * s + 4 * core + l
            one, two = pack.join(out[at], out[32 + at])
            chunk[s, l] = one
            chunk[s + 4, l] = two


def tiles(a):
    return a.reshape(-1, 32, 8, 2, 128).transpose(0, 1, 3, 2, 4).reshape(-1, 512, 128)


def body(ny, nz, start_states, labels):
    ns = lax.axis_size("space")
    s = lax.axis_index("space")
    y = lax.axis_index("y")
    quarter = lax.axis_index("zq")
    z = 2 * quarter + lax.axis_index("zp")
    core = lax.rem(s, 2)
    info = jnp.stack([core, s > 0, s < ns - 1, y * nz + z > 0, y, quarter, s, s]).astype(jnp.int32)
    swap = [(i, i ^ 1) for i in range(ns)]
    cross = [(i, i + 1) for i in range(1, ns - 1, 2)]
    cross = cross + [(b, a) for a, b in cross]

    def exchange(outer, inner):
        off = lax.ppermute(outer, "space", cross)
        on = lax.ppermute(inner, "space", swap)
        return off, on

    start = tiles(start_states.reshape(3, 512, 128))
    label = tiles(labels.reshape(1, 16 * NXB, 256))[0]
    layer = (2, 8, 256)
    vm = lambda *d: pltpu.VMEM(d, F32)
    window = shape(WN, *layer)
    edge = shape(HP, *layer)
    both = shape(3 * HS + HP, *layer)
    s_own, m_own, outer, inner = call(
        prepare,
        [shape(3, NXB, *layer), shape(NXB, *layer), both, both],
        [info, pltpu.with_memory_space_constraint(start, pltpu.HBM), pltpu.with_memory_space_constraint(label, pltpu.HBM)],
        [vm(3, 512, 128), pltpu.VMEM((512, 128), jnp.int32), vm(4, 256, 256), pltpu.SemaphoreType.DMA((4,))],
        ANY,
    )
    off, on = exchange(outer, inner)
    kept = [window, shape(6, WN, *layer), window, window, shape(CN, 8, 128), shape(6, CN, 8, 128), shape(CN, 8, 128)]
    kept.append(shape(3, WN, *layer))
    held = call(inside, kept, [info, s_own, m_own])
    coarse = [vm(CN, 8, 128)] * 3
    done = call(
        first_cycle,
        kept + [shape(3, NXB, *layer), window, shape(NXB, *layer), edge, edge, shape(3, 8, 8, 128)],
        [info, s_own, off, on] + list(held),
        [vm(3, NXB + 2 * HS, *layer), vm(WN, *layer)] + coarse + [vm(3, 12, 8, 128)] * 2,
        aliases={4 + i: i for i in range(8)},
    )
    held, (pred, tw, p1, outer, inner, gs) = done[:7], done[8:]
    off, on = exchange(outer, inner)
    base, send = call(
        second_cycle,
        [shape(3, NXB, *layer), shape(4, 4, 2, 5, 8, 128)],
        [info, pred, tw, p1, off, on, gs] + list(held),
        [vm(WN, *layer)] * 2 + coarse + [vm(256, 128)],
    )
    got = lax.all_to_all(send.reshape(ny * ns, 5, 8, 128), ("y", "space"), 0, 0)
    got = got.reshape(ny, ns, 5, 8, 128)
    swapped = lax.ppermute(got, "space", swap)
    acc, half, wa, wb = call(
        rows_scan,
        [shape(NC, 8, 128), shape(NC // 2, 8, 128), shape(NC, 8, 128), shape(NC, 8, 128)],
        [info, got, swapped],
        [vm(ROWS, 128)] * 2,
    )
    nt = ny * nz

    def shifted(value, k):
        return lax.ppermute(value, ("y", "zq", "zp"), [(i, i + k) for i in range(nt - k)])

    own = shifted(half, 1)
    other = lax.ppermute(own, "space", swap)
    state = [vm(ROWS, 128)] * 2
    acc, half = call(
        one_scan, [shape(NC, 8, 128), shape(NC // 2, 8, 128)], [info, acc, own, other, wa, wb], state
    )
    own = [shifted(half, k) for k in (2, 4, 6)]
    other = [lax.ppermute(part, "space", swap) for part in own]
    (chunks,) = call(
        even_scan, [shape(8, 4, 8, 128)], [info, acc] + own + other + [wa, wb], [vm(NC, 8, 128)] + state
    )
    (nat,) = call(interleave, [shape(3, 512, 128)], [base])
    back = lax.all_to_all(chunks, "space", 0, 0)
    w = back[:6].reshape(3, 8, 8, 128)
    (out,) = call(finish, [shape(3, 512, 128)], [nat, w], [vm(3, 512, 128), pltpu.SemaphoreType.DMA((3,))], VM, ANY)
    out = out.reshape(3, 32, 2, 8, 128).transpose(0, 1, 3, 2, 4)
    return out.reshape(1, 3, 16, NXB, 256)


def solution(mesh):
    nz = 8
    ny = mesh.shape["tm"] // nz
    split = Mesh(mesh.devices.reshape(ny, nz // 2, 2, mesh.shape["space"]), ("y", "zq", "zp", "space"))
    in_specs = (P(("y", "zq", "zp"), None, None, "space", None), P(None, "space", None))
    out_specs = P(("y", "zq", "zp"), None, None, "space", None)

    def run(start_states, labels):
        return body(ny, nz, start_states, labels)

    return jax.shard_map(run, mesh=split, in_specs=in_specs, out_specs=out_specs, check_vma=False)
```
